128 devices in a mesh: rows: 4 (over x), cols: 32 (over y, z, core).
Axes of the slice: x: 4, y: 4, z: 4, core: 2. Of those that a mesh axis runs over, the one named last changes fastest.
Arguments:
- weight: bfloat16 [8192, 16384], P('rows', 'cols'), may hold values from -0.046875 to 0.046875
- hess_inv: float32 [16384, 16384], P('rows', 'cols'), as said below
- selected: int32 [3, 64], replicated, may hold values from 0 to 16383, as said below
- block_mask: int32 [8192, 128], P('rows'), may hold values 0 or 1
- row_limits: int32 [8192], P('rows'), may hold values from 16 to 128
- calibration: bfloat16 [1024, 16384], P(None, 'cols'), may hold values from -6 to 6
Outputs:
- pruned: bfloat16 [8192, 16384], P('rows', 'cols')
- layer_error: float32 [8192, 1024], P('rows', 'cols')
The draws below stay inside these ranges and needn't reach their ends.
Inputs may be any that keep to these rules, and one draw needn't show every extreme that they name: `selected`: all 192 entries differ; 0 and 16383 are among them. `hess_inv`: symmetric positive definite.
All inputs are finite; a program needn't handle non-finite values. No bound on the sum of `block_mask` on one device may be relied on, other than what follows from the above.
Results may differ from the reference program's by a relative error of at most 0.005.
Values may be sent and summed in bfloat16 or wider, within the bound.
A program may use at most 128 MiB of HBM per device.

```python
import jax
import jax.numpy as jnp
from jax import lax

OUT = 8192
INPUTS = 16384
SEL = 64
STEPS = 3
BLK = 128
TOK = 1024
BLOCKS = 128


def draw_hess_inv(key, part):
    place_key, scale_key, damp_key = jax.random.split(jax.random.fold_in(key, 11), 3)
    places = jax.random.uniform(place_key, (INPUTS,), jnp.float32, 0.0, 1.0)
    scales = jax.random.uniform(scale_key, (INPUTS,), jnp.float32, 0.5, 1.5)
    damping = jax.random.uniform(damp_key, (INPUTS,), jnp.float32, 0.1, 0.4)
    reach = 1.0 / SEL
    gap = (places[:, None] - places[None, :]) * (1.0 / reach)
    kernel = scales[:, None] * scales[None, :] * jnp.exp(-0.5 * gap * gap)
    positions = jnp.arange(INPUTS)
    return jnp.where(positions[:, None] == positions[None, :], kernel + damping[:, None], kernel)


def draw_selected(key, part):
    inner_key = jax.random.fold_in(key, 5)
    middle = 1 + jax.random.permutation(inner_key, INPUTS - 2)[:STEPS * SEL - 2]
    joined = jnp.concatenate([jnp.zeros((1,), jnp.int32), middle.astype(jnp.int32), jnp.full((1,), INPUTS - 1, jnp.int32)])
    order = jax.random.permutation(jax.random.fold_in(key, 6), STEPS * SEL)
    return jnp.take(joined, order).reshape(STEPS, SEL)


def touch_ends(array, stream_key, least, top_value):
    spot = [jax.random.randint(jax.random.fold_in(stream_key, axis), (), 0, length) for axis, length in enumerate(array.shape)]
    longest = array.shape.index(max(array.shape))
    beside = spot[:longest] + [(spot[longest] + 1) % array.shape[longest]] + spot[longest + 1:]
    return array.at[tuple(spot)].set(least).at[tuple(beside)].set(top_value)


def shard_levels(rng, dims, shards, smallest, top_value):
    gain, own = 1.0, jax.random.fold_in(rng, 6)
    for axis_at, blocks in shards:
        draws = jnp.exp(jax.random.uniform(jax.random.fold_in(own, axis_at), (blocks,), jnp.float32, smallest / len(shards), top_value / len(shards)))
        gain = gain * jnp.repeat(draws, dims[axis_at] // blocks).reshape([-1 if axis == axis_at else 1 for axis in range(len(dims))])
    return gain


def noise(stream_key, shape, deviation, most, shards=(), kind=jnp.bfloat16):
    values = jax.random.normal(stream_key, shape, jnp.float32) * deviation
    if len(shards) > 0:
        values = shard_levels(stream_key, shape, shards, -0.22, 0.18) * values
    return jnp.clip(values, min=-most, max=most).astype(kind)


def setup_inputs(seed: int = 0) -> dict:
    seeds = jax.random.split(jax.random.key(seed), 7)
    return {
        "weight": noise(seeds[0], (OUT, INPUTS), INPUTS ** -0.5, 0.046875, ((0, 4), (1, 32))),
        "hess_inv": draw_hess_inv(jax.random.fold_in(seeds[6], 71), 0),
        "selected": draw_selected(jax.random.fold_in(seeds[6], 71), 0),
        "block_mask": touch_ends((jax.random.randint(seeds[3], (OUT, BLOCKS), 0, 4) < 3).astype(jnp.int32), jax.random.fold_in(seeds[3], 1), 0, 1),
        "row_limits": touch_ends(jax.random.randint(seeds[4], (OUT,), BLOCKS // 8, BLOCKS + 1), jax.random.fold_in(seeds[4], 1), BLOCKS // 8, BLOCKS).astype(jnp.int32),
        "calibration": noise(seeds[5], (TOK, INPUTS), 1.0, 6.0, ((1, 32),)),
    }


def reference(weight, hess_inv, selected, block_mask, row_limits, calibration):
    refit = weight.astype(jnp.float32)
    inverse = hess_inv
    for iteration in range(STEPS):
        chosen = selected[iteration]
        panel = jnp.take(inverse, chosen, axis=0)
        square = jnp.take(panel, chosen, axis=1)
        factor = jnp.linalg.cholesky(square)
        coeffs = jax.scipy.linalg.cho_solve((factor, True), panel)
        refit = refit - jnp.dot(jnp.take(refit, chosen, axis=1), coeffs, precision=lax.Precision.HIGHEST)
        inverse = inverse - jnp.dot(jnp.take(inverse, chosen, axis=1), coeffs, precision=lax.Precision.HIGHEST)
    running_count = jnp.cumsum(block_mask, axis=1)
    retained = block_mask * (running_count <= row_limits[:, None]).astype(jnp.int32)
    masked = (refit.reshape(OUT, BLOCKS, BLK) * retained.astype(jnp.float32)[:, :, None]).reshape(OUT, INPUTS)
    pruned = masked.astype(jnp.bfloat16)
    difference = (weight.astype(jnp.float32) - masked).astype(jnp.bfloat16)
    layer_error = lax.dot_general(difference.astype(jnp.float32), calibration.astype(jnp.float32), (((1,), (1,)), ((), ())), preferred_element_type=jnp.float32)
    return (pruned, layer_error)
```

```python
import jax
import jax.numpy as jnp
from jax import lax
from jax.sharding import PartitionSpec as P

BLK = 128


def local(weight, hess_inv, selected, block_mask, row_limits, calibration):
    rows_local, cols_local = hess_inv.shape
    out_local = weight.shape[0]
    group = lax.axis_size("cols")
    row_offset = lax.axis_index("rows") * rows_local
    col_offset = lax.axis_index("cols") * cols_local
    chosen = selected.reshape(-1)
    row_place = chosen - row_offset
    row_inside = (row_place >= 0) & (row_place < rows_local)
    own_rows = jnp.where(
        row_inside[:, None],
        jnp.take(hess_inv, jnp.clip(row_place, 0, rows_local - 1), axis=0),
        0.0,
    )
    onehot = (
        lax.broadcasted_iota(jnp.int32, (cols_local, chosen.shape[0]), 0) == (chosen - col_offset)[None, :]
    )
    square = lax.psum(
        jnp.dot(own_rows, onehot.astype(jnp.float32), precision=lax.Precision.HIGHEST), ("rows", "cols")
    )
    panel = lax.psum(own_rows, "rows")
    weight_cols = lax.psum(
        jnp.dot(weight, onehot.astype(jnp.bfloat16), preferred_element_type=jnp.float32).astype(jnp.bfloat16), "cols"
    )
    factor = jnp.linalg.cholesky(square)
    coeffs = jax.scipy.linalg.cho_solve((factor, True), panel)
    wide = weight.astype(jnp.float32)
    refit = wide - jnp.dot(weight_cols.astype(jnp.float32), coeffs, precision=lax.Precision.HIGHEST)
    blocks_local = cols_local // BLK
    running_count = jnp.cumsum(block_mask, axis=1)
    retained = block_mask * (running_count <= row_limits[:, None]).astype(jnp.int32)
    own_blocks = lax.dynamic_slice_in_dim(
        retained, lax.axis_index("cols") * blocks_local, blocks_local, 1
    )
    masked = (
        refit.reshape(out_local, blocks_local, BLK) * own_blocks.astype(jnp.float32)[:, :, None]
    ).reshape(out_local, cols_local)
    pruned = masked.astype(jnp.bfloat16)
    difference = (wide - masked).astype(jnp.bfloat16)
    tokens = calibration.shape[0]
    partial = lax.dot_general(
        calibration.reshape(group, tokens // group, cols_local),
        difference,
        (((2,), (1,)), ((), ())),
        preferred_element_type=jnp.float32,
    ).astype(jnp.bfloat16)
    pieces = lax.all_to_all(partial, "cols", split_axis=0, concat_axis=0, tiled=True)
    layer_error = jnp.sum(pieces.astype(jnp.float32), axis=0).T
    return (pruned, layer_error)


def solution(mesh):
    placed = (
        P("rows", "cols"),
        P("rows", "cols"),
        P(),
        P("rows", None),
        P("rows"),
        P(None, "cols"),
    )
    return jax.shard_map(
        local,
        mesh=mesh,
        in_specs=placed,
        out_specs=(P("rows", "cols"), P("rows", "cols")),
        check_vma=False,
    )
```

```python
import functools

import jax
import jax.numpy as jnp
from jax import lax
from jax.experimental import pallas as pl
from jax.experimental.pallas import tpu as pltpu
from jax.sharding import PartitionSpec as P

BLK = 128
LANES = 256
MESH = pl.DeviceIdType.MESH
HIGHEST = lax.Precision.HIGHEST


def aligned(value, factor):
    return pl.multiple_of(value, factor)


def place():
    row = lax.axis_index("rows")
    col = lax.axis_index("cols")
    core = lax.rem(col, 2)
    z = lax.rem(col // 2, 4)
    y = col // 8
    partner = (row, col + 1 - 2 * core)
    axes = {
        "x": (row, lambda j: (j, col)),
        "y": (y, lambda j: (row, (j * 4 + z) * 2 + core)),
        "z": (z, lambda j: (row, (y * 4 + j) * 2 + core)),
    }
    return core, partner, axes


def enter(partner, axes):
    barrier = pltpu.get_barrier_semaphore()
    pl.semaphore_signal(barrier, inc=1, device_id=partner, device_id_type=MESH)
    for index, device in axes.values():
        for step in (1, 2, 3):
            pl.semaphore_signal(
                barrier, inc=1, device_id=device(lax.rem(index + step, 4)), device_id_type=MESH
            )
    pl.semaphore_wait(barrier, 1 + 3 * len(axes))


def exchange_kernel(
    own_ref, weight_ref, line_ref, square_ref, panel_ref, chosen_ref,
    square_part, half_rx, half, z_rx, z_sum, y_rx, y_sum, x_rx,
    panel_rx, weight_part, weight_rx, weight_half, first_rx, first_sum, second_rx,
    send_sem, recv_sem,
):
    core, partner, axes = place()
    col_offset = lax.axis_index("cols") * weight_ref.shape[1]
    count = own_ref.shape[0]
    half_rows = count // 2
    quarter = half_rows // 4
    started = []

    def send(src, dst, stage, slot, device):
        copy = pltpu.make_async_remote_copy(
            src_ref=src, dst_ref=dst, send_sem=send_sem.at[stage, slot], recv_sem=recv_sem.at[stage, slot],
            device_id=device, device_id_type=MESH,
        )
        copy.start()
        started.append(copy)
        return copy

    def scatter(axis, src, base, piece, rx, stage):
        index, device = axes[axis]
        copies = []
        for step in (1, 2, 3):
            peer = lax.rem(index + step, 4)
            start = aligned(base + peer * piece, 8)
            copies.append(send(src.at[pl.ds(start, piece)], rx.at[step - 1], stage, step - 1, device(peer)))
        return copies

    def spread(axis, src, dst_of, stage):
        index, device = axes[axis]
        return [
            send(src, dst_of(step - 1), stage, step - 1, device(lax.rem(index + step, 4))) for step in (1, 2, 3)
        ]

    def arrive(copies):
        for copy in copies:
            copy.wait_recv()

    def total(own, rx):
        return own + rx[0] + rx[1] + rx[2]

    enter(partner, axes)

    x, y, z = axes["x"][0], axes["y"][0], axes["z"][0]
    lines = lax.broadcasted_iota(jnp.int32, (weight_ref.shape[1], LANES), 0) + col_offset
    onehot = jnp.where(lines == line_ref[0:1, :], 1.0, 0.0)
    square_part[...] = jnp.dot(own_ref[...], onehot, precision=HIGHEST, preferred_element_type=jnp.float32)
    s1 = send(
        square_part.at[pl.ds(aligned((1 - core) * half_rows, 8), half_rows)], half_rx, 0, 0, partner
    )
    panel_piece = count // 4
    p1 = scatter("x", own_ref, 0, panel_piece, panel_rx, 1)
    weight_part[...] = jnp.dot(
        weight_ref[...], onehot.astype(jnp.bfloat16), preferred_element_type=jnp.float32
    ).astype(jnp.bfloat16)
    rows = weight_ref.shape[0]
    share = rows // 2
    w1 = send(weight_part.at[pl.ds(aligned((1 - core) * share, 16), share)], weight_rx, 2, 0, partner)
    s1.wait_recv()
    half[...] = square_part[pl.ds(aligned(core * half_rows, 8), half_rows), :] + half_rx[...]
    s2 = scatter("z", half, 0, quarter, z_rx, 3)
    arrive(s2)
    z_sum[...] = total(half[pl.ds(aligned(z * quarter, 8), quarter), :], z_rx)
    s3 = spread("y", z_sum, lambda slot: y_rx.at[slot], 4)
    w1.wait_recv()
    weight_half[...] = weight_part[pl.ds(aligned(core * share, 16), share), :] + weight_rx[...]
    arrive(s3)
    y_sum[...] = total(z_sum[...], y_rx)
    s4 = spread("x", y_sum, lambda slot: x_rx.at[slot], 5)
    part = share // 2
    piece = part // 4
    small = piece // 4
    wa = scatter("y", weight_half, 0, piece, first_rx.at[0], 6)
    wb = scatter("z", weight_half, part, piece, first_rx.at[1], 7)
    arrive(s4)
    mine = pl.ds(aligned(core * half_rows + z * quarter, 8), quarter)
    square_ref[mine, :] = total(y_sum[...], x_rx)
    s5 = spread("z", square_ref.at[mine], lambda slot: square_ref.at[mine], 8)
    arrive(p1)
    own_panel = pl.ds(aligned(x * panel_piece, 8), panel_piece)
    panel_ref[own_panel, :] = total(own_ref[own_panel, :], panel_rx)
    p2 = spread("x", panel_ref.at[own_panel], lambda slot: panel_ref.at[own_panel], 9)
    arrive(s5)
    own_half = pl.ds(aligned(core * half_rows, 8), half_rows)
    s6 = send(square_ref.at[own_half], square_ref.at[own_half], 10, 0, partner)
    arrive(wa)
    first_sum[0] = total(weight_half[pl.ds(aligned(y * piece, 16), piece), :], first_rx.at[0])
    wa = scatter("z", first_sum.at[0], 0, small, second_rx.at[0], 11)
    arrive(wb)
    first_sum[1] = total(weight_half[pl.ds(aligned(part + z * piece, 16), piece), :], first_rx.at[1])
    wb = scatter("y", first_sum.at[1], 0, small, second_rx.at[1], 12)
    arrive(wa)
    base_a = core * share + y * piece
    base_b = core * share + part + z * piece
    slice_a = pl.ds(aligned(base_a + z * small, 16), small)
    slice_b = pl.ds(aligned(base_b + y * small, 16), small)
    chosen_ref[slice_a, :] = total(first_sum[0, pl.ds(aligned(z * small, 16), small), :], second_rx.at[0])
    wa = spread("z", chosen_ref.at[slice_a], lambda slot: chosen_ref.at[slice_a], 13)
    arrive(wb)
    chosen_ref[slice_b, :] = total(first_sum[1, pl.ds(aligned(y * small, 16), small), :], second_rx.at[1])
    wb = spread("y", chosen_ref.at[slice_b], lambda slot: chosen_ref.at[slice_b], 14)
    arrive(wa)
    piece_a = pl.ds(aligned(base_a, 16), piece)
    wa = spread("y", chosen_ref.at[piece_a], lambda slot: chosen_ref.at[piece_a], 15)
    arrive(wb)
    piece_b = pl.ds(aligned(base_b, 16), piece)
    wb = spread("z", chosen_ref.at[piece_b], lambda slot: chosen_ref.at[piece_b], 16)
    arrive(wa)
    arrive(wb)
    own_share = pl.ds(aligned(core * share, 16), share)
    w6 = send(chosen_ref.at[own_share], chosen_ref.at[own_share], 17, 0, partner)
    arrive(p2)
    s6.wait_recv()
    w6.wait_recv()
    for copy in started:
        copy.wait_send()


def exchange(own_rows, weight, line):
    count, columns = own_rows.shape
    rows = weight.shape[0]
    f32, bf16 = jnp.float32, jnp.bfloat16
    half, quarter = count // 2, count // 8
    share = rows // 2
    piece = share // 8
    small = piece // 4
    vmem = pl.BlockSpec(memory_space=pltpu.VMEM)
    return pl.pallas_call(
        exchange_kernel,
        out_shape=(
            jax.ShapeDtypeStruct((count, LANES), f32),
            jax.ShapeDtypeStruct((count, columns), f32),
            jax.ShapeDtypeStruct((rows, LANES), bf16),
        ),
        in_specs=[vmem] * 3,
        out_specs=(vmem,) * 3,
        scratch_shapes=[
            pltpu.VMEM((count, LANES), f32),
            pltpu.VMEM((half, LANES), f32),
            pltpu.VMEM((half, LANES), f32),
            pltpu.VMEM((3, quarter, LANES), f32),
            pltpu.VMEM((quarter, LANES), f32),
            pltpu.VMEM((3, quarter, LANES), f32),
            pltpu.VMEM((quarter, LANES), f32),
            pltpu.VMEM((3, quarter, LANES), f32),
            pltpu.VMEM((3, count // 4, columns), f32),
            pltpu.VMEM((rows, LANES), bf16),
            pltpu.VMEM((share, LANES), bf16),
            pltpu.VMEM((share, LANES), bf16),
            pltpu.VMEM((2, 3, piece, LANES), bf16),
            pltpu.VMEM((2, piece, LANES), bf16),
            pltpu.VMEM((2, 3, small, LANES), bf16),
            pltpu.SemaphoreType.DMA((18, 3)),
            pltpu.SemaphoreType.DMA((18, 3)),
        ],
        compiler_params=pltpu.CompilerParams(
            collective_id=0, has_side_effects=True, vmem_limit_bytes=40 << 20
        ),
        name="exchange",
    )(own_rows, weight, line)


def invert_kernel(square_ref, panel_ref, coeffs_ref, state):
    count = square_ref.shape[0]
    side = 64
    state[...] = square_ref[...]
    lane = lax.broadcasted_iota(jnp.int32, (side, BLK), 1)
    line = lax.broadcasted_iota(jnp.int32, (side, BLK), 0)
    for block in range(count // side):
        lo = block * side
        tile = state[lo : lo + side, (lo // BLK) * BLK : (lo // BLK) * BLK + BLK]
        shift = lo % BLK
        for k in range(side):
            pivot_row = tile[k : k + 1, :]
            column = jnp.take_along_axis(tile, jnp.full((side, BLK), k + shift, jnp.int32), axis=1)
            scale = 1.0 / column[k : k + 1, :]
            scaled = jnp.where(lane[0:1, :] == k + shift, scale, pivot_row * scale)
            kept = jnp.where(lane == k + shift, 0.0, tile)
            tile = jnp.where(line == k, scaled, kept - column * scaled)
        inverse = tile[:, shift : shift + side]
        strip = state[:, lo : lo + side]
        lanes = lax.broadcasted_iota(jnp.int32, (side, LANES), 1)
        inside = (lanes >= lo) & (lanes < lo + side)
        unit = jnp.where(lanes - lo == lax.broadcasted_iota(jnp.int32, (side, LANES), 0), 1.0, 0.0)
        right = jnp.where(inside, unit, state[lo : lo + side, :])
        right = jnp.dot(inverse, right, precision=HIGHEST, preferred_element_type=jnp.float32)
        all_lanes = lax.broadcasted_iota(jnp.int32, (count, LANES), 1)
        cleared = jnp.where((all_lanes >= lo) & (all_lanes < lo + side), 0.0, state[...])
        state[...] = cleared - jnp.dot(strip, right, precision=HIGHEST, preferred_element_type=jnp.float32)
        state[lo : lo + side, :] = right
    coeffs_ref[...] = jnp.dot(
        state[:, :count], panel_ref[...], precision=HIGHEST, preferred_element_type=jnp.float32
    )


def solve(square, panel):
    return pl.pallas_call(
        invert_kernel,
        out_shape=jax.ShapeDtypeStruct(panel.shape, jnp.float32),
        in_specs=[pl.BlockSpec(memory_space=pltpu.VMEM)] * 2,
        out_specs=pl.BlockSpec(memory_space=pltpu.VMEM),
        scratch_shapes=[pltpu.VMEM(square.shape, jnp.float32)],
        name="solve",
    )(square, panel)


def local(weight, hess_inv, selected, block_mask, row_limits, calibration):
    rows_local, cols_local = hess_inv.shape
    out_local = weight.shape[0]
    group = lax.axis_size("cols")
    row_offset = lax.axis_index("rows") * rows_local
    chosen = selected.reshape(-1)
    count = chosen.shape[0]
    row_place = chosen - row_offset
    row_inside = (row_place >= 0) & (row_place < rows_local)
    own_rows = jnp.where(
        row_inside[:, None],
        jnp.take(hess_inv, jnp.clip(row_place, 0, rows_local - 1), axis=0),
        0.0,
    )
    line = jnp.broadcast_to(jnp.pad(chosen, (0, LANES - count), constant_values=-1)[None, :], (8, LANES))
    square, panel, weight_cols = exchange(own_rows, weight, line)
    coeffs = solve(square, panel)
    wide = weight.astype(jnp.float32)
    refit = wide - jnp.dot(weight_cols[:, :count].astype(jnp.float32), coeffs, precision=HIGHEST)
    blocks_local = cols_local // BLK
    running_count = jnp.cumsum(block_mask, axis=1)
    retained = block_mask * (running_count <= row_limits[:, None]).astype(jnp.int32)
    own_blocks = lax.dynamic_slice_in_dim(
        retained, lax.axis_index("cols") * blocks_local, blocks_local, 1
    )
    masked = (
        refit.reshape(out_local, blocks_local, BLK) * own_blocks.astype(jnp.float32)[:, :, None]
    ).reshape(out_local, cols_local)
    pruned = masked.astype(jnp.bfloat16)
    difference = (wide - masked).astype(jnp.bfloat16)
    tokens = calibration.shape[0]
    partial = lax.dot_general(
        calibration.reshape(group, tokens // group, cols_local),
        difference,
        (((2,), (1,)), ((), ())),
        preferred_element_type=jnp.float32,
    ).astype(jnp.bfloat16)
    pieces = lax.all_to_all(partial, "cols", split_axis=0, concat_axis=0, tiled=True)
    layer_error = jnp.sum(pieces.astype(jnp.float32), axis=0).T
    return (pruned, layer_error)


def solution(mesh):
    placed = (
        P("rows", "cols"),
        P("rows", "cols"),
        P(),
        P("rows", None),
        P("rows"),
        P(None, "cols"),
    )
    return jax.shard_map(
        local,
        mesh=mesh,
        in_specs=placed,
        out_specs=(P("rows", "cols"), P("rows", "cols")),
        check_vma=False,
    )
```

```python
import functools

import jax
import jax.numpy as jnp
from jax import lax
from jax.experimental import pallas as pl
from jax.experimental.pallas import tpu as pltpu
from jax.sharding import PartitionSpec as P

BLK = 128
LANES = 256
MESH = pl.DeviceIdType.MESH
HIGHEST = lax.Precision.HIGHEST


def aligned(value, factor):
    return pl.multiple_of(value, factor)


def place():
    row = lax.axis_index("rows")
    col = lax.axis_index("cols")
    core = lax.rem(col, 2)
    z = lax.rem(col // 2, 4)
    y = col // 8
    partner = (row, col + 1 - 2 * core)
    axes = {
        "x": (row, lambda j: (j, col)),
        "y": (y, lambda j: (row, (j * 4 + z) * 2 + core)),
        "z": (z, lambda j: (row, (y * 4 + j) * 2 + core)),
    }
    return core, partner, axes


def enter(partner, axes):
    barrier = pltpu.get_barrier_semaphore()
    pl.semaphore_signal(barrier, inc=1, device_id=partner, device_id_type=MESH)
    for index, device in axes.values():
        for step in (1, 2, 3):
            pl.semaphore_signal(
                barrier, inc=1, device_id=device(lax.rem(index + step, 4)), device_id_type=MESH
            )
    pl.semaphore_wait(barrier, 1 + 3 * len(axes))


def exchange_kernel(
    own_ref, weight_ref, line_ref, square_ref, panel_ref, chosen_ref,
    square_part, half_rx, half, z_rx, z_sum, y_rx, y_sum, x_rx,
    panel_rx, weight_part, weight_rx, weight_half, first_rx, first_sum, second_rx,
    send_sem, recv_sem,
):
    core, partner, axes = place()
    col_offset = lax.axis_index("cols") * weight_ref.shape[1]
    count = own_ref.shape[0]
    half_rows = count // 2
    quarter = half_rows // 4
    started = []

    def send(src, dst, stage, slot, device):
        copy = pltpu.make_async_remote_copy(
            src_ref=src, dst_ref=dst, send_sem=send_sem.at[stage, slot], recv_sem=recv_sem.at[stage, slot],
            device_id=device, device_id_type=MESH,
        )
        copy.start()
        started.append(copy)
        return copy

    def scatter(axis, src, base, piece, rx, stage):
        index, device = axes[axis]
        copies = []
        for step in (1, 2, 3):
            peer = lax.rem(index + step, 4)
            start = aligned(base + peer * piece, 8)
            copies.append(send(src.at[pl.ds(start, piece)], rx.at[step - 1], stage, step - 1, device(peer)))
        return copies

    def spread(axis, src, dst_of, stage):
        index, device = axes[axis]
        return [
            send(src, dst_of(step - 1), stage, step - 1, device(lax.rem(index + step, 4))) for step in (1, 2, 3)
        ]

    def arrive(copies):
        for copy in copies:
            copy.wait_recv()

    def total(own, rx):
        return own + rx[0] + rx[1] + rx[2]

    enter(partner, axes)

    x, y, z = axes["x"][0], axes["y"][0], axes["z"][0]
    lines = lax.broadcasted_iota(jnp.int32, (weight_ref.shape[1], LANES), 0) + col_offset
    onehot = jnp.where(lines == line_ref[0:1, :], 1.0, 0.0)
    square_part[...] = jnp.dot(own_ref[...], onehot, precision=HIGHEST, preferred_element_type=jnp.float32)
    s1 = send(
        square_part.at[pl.ds(aligned((1 - core) * half_rows, 8), half_rows)], half_rx, 0, 0, partner
    )
    panel_piece = count // 4
    p1 = scatter("x", own_ref, 0, panel_piece, panel_rx, 1)
    weight_part[...] = jnp.dot(
        weight_ref[...], onehot.astype(jnp.bfloat16), preferred_element_type=jnp.float32
    ).astype(jnp.bfloat16)
    rows = weight_ref.shape[0]
    share = rows // 2
    w1 = send(weight_part.at[pl.ds(aligned((1 - core) * share, 16), share)], weight_rx, 2, 0, partner)
    s1.wait_recv()
    half[...] = square_part[pl.ds(aligned(core * half_rows, 8), half_rows), :] + half_rx[...]
    s2 = scatter("z", half, 0, quarter, z_rx, 3)
    arrive(s2)
    z_sum[...] = total(half[pl.ds(aligned(z * quarter, 8), quarter), :], z_rx)
    s3 = spread("y", z_sum, lambda slot: y_rx.at[slot], 4)
    w1.wait_recv()
    weight_half[...] = weight_part[pl.ds(aligned(core * share, 16), share), :] + weight_rx[...]
    arrive(s3)
    y_sum[...] = total(z_sum[...], y_rx)
    s4 = spread("x", y_sum, lambda slot: x_rx.at[slot], 5)
    part = share // 2
    piece = part // 4
    small = piece // 4
    wa = scatter("y", weight_half, 0, piece, first_rx.at[0], 6)
    wb = scatter("z", weight_half, part, piece, first_rx.at[1], 7)
    arrive(s4)
    mine = pl.ds(aligned(core * half_rows + z * quarter, 8), quarter)
    square_ref[mine, :] = total(y_sum[...], x_rx)
    s5 = spread("z", square_ref.at[mine], lambda slot: square_ref.at[mine], 8)
    arrive(p1)
    own_panel = pl.ds(aligned(x * panel_piece, 8), panel_piece)
    panel_ref[own_panel, :] = total(own_ref[own_panel, :], panel_rx)
    p2 = spread("x", panel_ref.at[own_panel], lambda slot: panel_ref.at[own_panel], 9)
    arrive(s5)
    own_half = pl.ds(aligned(core * half_rows, 8), half_rows)
    s6 = send(square_ref.at[own_half], square_ref.at[own_half], 10, 0, partner)
    arrive(wa)
    first_sum[0] = total(weight_half[pl.ds(aligned(y * piece, 16), piece), :], first_rx.at[0])
    wa = scatter("z", first_sum.at[0], 0, small, second_rx.at[0], 11)
    arrive(wb)
    first_sum[1] = total(weight_half[pl.ds(aligned(part + z * piece, 16), piece), :], first_rx.at[1])
    wb = scatter("y", first_sum.at[1], 0, small, second_rx.at[1], 12)
    arrive(wa)
    base_a = core * share + y * piece
    base_b = core * share + part + z * piece
    slice_a = pl.ds(aligned(base_a + z * small, 16), small)
    slice_b = pl.ds(aligned(base_b + y * small, 16), small)
    chosen_ref[slice_a, :] = total(first_sum[0, pl.ds(aligned(z * small, 16), small), :], second_rx.at[0])
    wa = spread("z", chosen_ref.at[slice_a], lambda slot: chosen_ref.at[slice_a], 13)
    arrive(wb)
    chosen_ref[slice_b, :] = total(first_sum[1, pl.ds(aligned(y * small, 16), small), :], second_rx.at[1])
    wb = spread("y", chosen_ref.at[slice_b], lambda slot: chosen_ref.at[slice_b], 14)
    arrive(wa)
    piece_a = pl.ds(aligned(base_a, 16), piece)
    wa = spread("y", chosen_ref.at[piece_a], lambda slot: chosen_ref.at[piece_a], 15)
    arrive(wb)
    piece_b = pl.ds(aligned(base_b, 16), piece)
    wb = spread("z", chosen_ref.at[piece_b], lambda slot: chosen_ref.at[piece_b], 16)
    arrive(wa)
    arrive(wb)
    own_share = pl.ds(aligned(core * share, 16), share)
    w6 = send(chosen_ref.at[own_share], chosen_ref.at[own_share], 17, 0, partner)
    arrive(p2)
    s6.wait_recv()
    w6.wait_recv()
    for copy in started:
        copy.wait_send()


def exchange(own_rows, weight, line):
    count, columns = own_rows.shape
    rows = weight.shape[0]
    f32, bf16 = jnp.float32, jnp.bfloat16
    half, quarter = count // 2, count // 8
    share = rows // 2
    piece = share // 8
    small = piece // 4
    vmem = pl.BlockSpec(memory_space=pltpu.VMEM)
    return pl.pallas_call(
        exchange_kernel,
        out_shape=(
            jax.ShapeDtypeStruct((count, LANES), f32),
            jax.ShapeDtypeStruct((count, columns), f32),
            jax.ShapeDtypeStruct((rows, LANES), bf16),
        ),
        in_specs=[vmem] * 3,
        out_specs=(vmem,) * 3,
        scratch_shapes=[
            pltpu.VMEM((count, LANES), f32),
            pltpu.VMEM((half, LANES), f32),
            pltpu.VMEM((half, LANES), f32),
            pltpu.VMEM((3, quarter, LANES), f32),
            pltpu.VMEM((quarter, LANES), f32),
            pltpu.VMEM((3, quarter, LANES), f32),
            pltpu.VMEM((quarter, LANES), f32),
            pltpu.VMEM((3, quarter, LANES), f32),
            pltpu.VMEM((3, count // 4, columns), f32),
            pltpu.VMEM((rows, LANES), bf16),
            pltpu.VMEM((share, LANES), bf16),
            pltpu.VMEM((share, LANES), bf16),
            pltpu.VMEM((2, 3, piece, LANES), bf16),
            pltpu.VMEM((2, piece, LANES), bf16),
            pltpu.VMEM((2, 3, small, LANES), bf16),
            pltpu.SemaphoreType.DMA((18, 3)),
            pltpu.SemaphoreType.DMA((18, 3)),
        ],
        compiler_params=pltpu.CompilerParams(
            collective_id=0, has_side_effects=True, vmem_limit_bytes=40 << 20
        ),
        name="exchange",
    )(own_rows, weight, line)


def invert_kernel(square_ref, panel_ref, coeffs_ref, state):
    count = square_ref.shape[0]
    side = 64
    state[...] = square_ref[...]
    lane = lax.broadcasted_iota(jnp.int32, (side, BLK), 1)
    line = lax.broadcasted_iota(jnp.int32, (side, BLK), 0)
    for block in range(count // side):
        lo = block * side
        tile = state[lo : lo + side, (lo // BLK) * BLK : (lo // BLK) * BLK + BLK]
        shift = lo % BLK
        for k in range(side):
            pivot_row = tile[k : k + 1, :]
            column = jnp.take_along_axis(tile, jnp.full((side, BLK), k + shift, jnp.int32), axis=1)
            scale = 1.0 / column[k : k + 1, :]
            scaled = jnp.where(lane[0:1, :] == k + shift, scale, pivot_row * scale)
            kept = jnp.where(lane == k + shift, 0.0, tile)
            tile = jnp.where(line == k, scaled, kept - column * scaled)
        inverse = tile[:, shift : shift + side]
        strip = state[:, lo : lo + side]
        lanes = lax.broadcasted_iota(jnp.int32, (side, LANES), 1)
        inside = (lanes >= lo) & (lanes < lo + side)
        unit = jnp.where(lanes - lo == lax.broadcasted_iota(jnp.int32, (side, LANES), 0), 1.0, 0.0)
        right = jnp.where(inside, unit, state[lo : lo + side, :])
        right = jnp.dot(inverse, right, precision=HIGHEST, preferred_element_type=jnp.float32)
        all_lanes = lax.broadcasted_iota(jnp.int32, (count, LANES), 1)
        cleared = jnp.where((all_lanes >= lo) & (all_lanes < lo + side), 0.0, state[...])
        state[...] = cleared - jnp.dot(strip, right, precision=HIGHEST, preferred_element_type=jnp.float32)
        state[lo : lo + side, :] = right
    coeffs_ref[...] = jnp.dot(
        state[:, :count], panel_ref[...], precision=HIGHEST, preferred_element_type=jnp.float32
    )


def solve(square, panel):
    return pl.pallas_call(
        invert_kernel,
        out_shape=jax.ShapeDtypeStruct(panel.shape, jnp.float32),
        in_specs=[pl.BlockSpec(memory_space=pltpu.VMEM)] * 2,
        out_specs=pl.BlockSpec(memory_space=pltpu.VMEM),
        scratch_shapes=[pltpu.VMEM(square.shape, jnp.float32)],
        name="solve",
    )(square, panel)


def reduce_kernel(
    weight_ref, chosen_ref, coeffs_ref, mask_ref, limit_ref, features_ref, pruned_ref, error_ref,
    high, low, features_rx, own_diff, sent_diff, diff_rx, part, forward_rx, forward, ring_rx,
    sums, sums_wide, small_forward_rx, small_forward, small_rx, final,
    send_sem, recv_sem,
):
    core, partner, axes = place()
    axes = {name: axes[name] for name in ("y", "z")}
    rows, columns = weight_ref.shape
    share = rows // 2
    chunks = part.shape[0]
    chunk = share // chunks
    blocks = columns // BLK
    tokens_axis = part.shape[1]
    first_block = lax.axis_index("cols") * blocks
    started = []

    def remote(src, dst, stage, slot, device):
        return pltpu.make_async_remote_copy(
            src_ref=src, dst_ref=dst, send_sem=send_sem.at[stage, slot], recv_sem=recv_sem.at[stage, slot],
            device_id=device, device_id_type=MESH,
        )

    def send(*args):
        copy = remote(*args)
        copy.start()
        started.append(copy)
        return copy

    enter(partner, axes)
    features_copy = send(features_ref, features_rx, 0, 0, partner)

    coeffs = coeffs_ref[...]
    high[...] = coeffs.astype(jnp.bfloat16)
    low[...] = (coeffs - high[...].astype(jnp.float32)).astype(jnp.bfloat16)
    count = coeffs_ref.shape[0]
    line = lax.broadcasted_iota(jnp.int32, (BLK, columns), 0)
    block = first_block + lax.broadcasted_iota(jnp.int32, (BLK, columns), 1) // BLK
    before = jnp.where(line <= block, 1.0, 0.0).astype(jnp.bfloat16)
    here = jnp.where(line == block, 1.0, 0.0).astype(jnp.bfloat16)
    spread = jnp.where(lax.broadcasted_iota(jnp.int32, (16, columns), 0) == 0, 1.0, 0.0).astype(jnp.bfloat16)

    def differ(first, store):
        lines = pl.ds(aligned(first, chunk), chunk)
        picked = chosen_ref[lines, :][:, :count]
        change = jnp.dot(picked, high[...], preferred_element_type=jnp.float32)
        change += jnp.dot(picked, low[...], preferred_element_type=jnp.float32)
        mask = mask_ref[lines, :].astype(jnp.float32).astype(jnp.bfloat16)
        seen = jnp.dot(mask, before, preferred_element_type=jnp.float32)
        bit = jnp.dot(mask, here, preferred_element_type=jnp.float32)
        limit = lax.dot_general(
            limit_ref[:, lines], spread, (((0,), (0,)), ((), ())), preferred_element_type=jnp.float32
        )
        kept = jnp.where(seen <= limit, bit, 0.0)
        wide = weight_ref[lines, :].astype(jnp.float32)
        masked = (wide - change) * kept
        pruned_ref[lines, :] = masked.astype(jnp.bfloat16)
        store((wide - masked).astype(jnp.bfloat16))

    def diff_copy(i):
        lines = pl.ds(aligned(i * chunk, chunk), chunk)
        return remote(sent_diff.at[lines], diff_rx.at[lines], 1, i, partner)

    @pl.loop(0, chunks)
    def _(i):
        def store(value):
            sent_diff[pl.ds(aligned(i * chunk, chunk), chunk), :] = value

        differ((1 - core) * share + i * chunk, store)
        diff_copy(i).start()

    @pl.loop(0, chunks)
    def _(i):
        def store(value):
            own_diff[pl.ds(aligned(i * chunk, chunk), chunk), :] = value

        differ(core * share + i * chunk, store)

    features_copy.wait_recv()

    def multiply(k):
        lines = pl.ds(k * chunk, chunk)
        tokens = features_ref.shape[0] // tokens_axis

        @pl.loop(0, tokens_axis)
        def _(t):
            words = pl.ds(aligned(t * tokens, tokens), tokens)
            product = lax.dot_general(
                features_ref[words, :], own_diff[lines, :], (((1,), (1,)), ((), ())),
                preferred_element_type=jnp.float32,
            )
            product += lax.dot_general(
                features_rx[words, :], diff_rx[lines, :], (((1,), (1,)), ((), ())),
                preferred_element_type=jnp.float32,
            )
            part[k, t] = product.astype(jnp.bfloat16).reshape(part.shape[2:])

    def ring(axis, sent, value, extent, through_rx, through, rx, stage):
        index, device = axes[axis]
        right, left, across = lax.rem(index + 1, 4), lax.rem(index + 3, 4), lax.rem(index + 2, 4)
        lo, hi = pl.ds(0, extent // 2), pl.ds(extent // 2, extent // 2)
        a = send(sent(across).at[lo], through_rx.at[0], stage, 0, device(right))
        b = send(sent(across).at[hi], through_rx.at[1], stage, 1, device(left))
        c = send(sent(right).at[hi], rx.at[0, hi], stage, 2, device(right))
        d = send(sent(left).at[lo], rx.at[1, lo], stage, 3, device(left))
        later = []

        def pass_on():
            a.wait_recv()
            through[0] = (value(right, lo) + through_rx[0].astype(jnp.float32)).astype(jnp.bfloat16)
            later.append(send(through.at[0], rx.at[0, lo], stage, 4, device(right)))
            b.wait_recv()
            through[1] = (value(left, hi) + through_rx[1].astype(jnp.float32)).astype(jnp.bfloat16)
            later.append(send(through.at[1], rx.at[1, hi], stage, 5, device(left)))

        def finish():
            for copy in (c, d, *later):
                copy.wait_recv()
            return value(index, pl.ds(0, extent)) + rx[0].astype(jnp.float32) + rx[1].astype(jnp.float32)

        return pass_on, finish

    order = [k for pair in zip(range(chunks // 2), range(chunks // 2, chunks)) for k in pair]
    rings = {}
    for k in order:
        diff_copy(k).wait_recv()
        multiply(k)
        if k < chunks // 2:
            axis = "y"
            sent = functools.partial(lambda k, j: part.at[k, j], k)
        else:
            axis = "z"
            sent = functools.partial(lambda k, j: part.at[k, :, j], k)
        value = functools.partial(lambda sent, j, which: sent(j).at[which][...].astype(jnp.float32), sent)
        rings[k] = ring(axis, sent, value, 4, forward_rx.at[k], forward.at[k], ring_rx.at[k], 2 + k)
    for k in order:
        rings[k][0]()
    again = {}
    for k in order:
        total = rings[k][1]()
        sums_wide[k] = total
        sums[k] = total.astype(jnp.bfloat16)
        axis = "z" if k < chunks // 2 else "y"
        sent = functools.partial(lambda k, j: sums.at[k, j], k)
        value = functools.partial(lambda k, j, which: sums_wide[k, j, which, :], k)
        again[k] = ring(
            axis, sent, value, 64, small_forward_rx.at[k], small_forward.at[k], small_rx.at[k], 2 + chunks + k
        )
    for k in order:
        again[k][0]()
    tokens = error_ref.shape[0]
    last = []
    for k in order:
        final[k] = again[k][1]()
        lanes = pl.ds(aligned(core * share + k * chunk, chunk), chunk)
        last.append(
            send(
                final.at[k, pl.ds(aligned((1 - core) * tokens, tokens), tokens)],
                error_ref.at[:, lanes], 2 + 2 * chunks, k, partner,
            )
        )
        error_ref[:, lanes] = final[k, pl.ds(aligned(core * tokens, tokens), tokens), :]
    for copy in last:
        copy.wait_recv()
    for i in range(chunks):
        diff_copy(i).wait_send()
    for copy in started:
        copy.wait_send()


def reduce_error(weight, chosen, coeffs, mask, limit, features):
    rows, columns = weight.shape
    tokens = features.shape[0]
    f32, bf16 = jnp.float32, jnp.bfloat16
    share, chunks = rows // 2, 4
    chunk = share // chunks
    vmem = pl.BlockSpec(memory_space=pltpu.VMEM)
    return pl.pallas_call(
        reduce_kernel,
        out_shape=(
            jax.ShapeDtypeStruct((rows, columns), bf16),
            jax.ShapeDtypeStruct((tokens // 32, rows), f32),
        ),
        in_specs=[vmem] * 6,
        out_specs=(vmem,) * 2,
        scratch_shapes=[
            pltpu.VMEM(coeffs.shape, bf16),
            pltpu.VMEM(coeffs.shape, bf16),
            pltpu.VMEM(features.shape, bf16),
            pltpu.VMEM((share, columns), bf16),
            pltpu.VMEM((share, columns), bf16),
            pltpu.VMEM((share, columns), bf16),
            pltpu.VMEM((chunks, 4, 4, 64, chunk), bf16),
            pltpu.VMEM((chunks, 2, 2, 64, chunk), bf16),
            pltpu.VMEM((chunks, 2, 2, 64, chunk), bf16),
            pltpu.VMEM((chunks, 2, 4, 64, chunk), bf16),
            pltpu.VMEM((chunks, 4, 64, chunk), bf16),
            pltpu.VMEM((chunks, 4, 64, chunk), f32),
            pltpu.VMEM((chunks, 2, 32, chunk), bf16),
            pltpu.VMEM((chunks, 2, 32, chunk), bf16),
            pltpu.VMEM((chunks, 2, 64, chunk), bf16),
            pltpu.VMEM((chunks, 64, chunk), f32),
            pltpu.SemaphoreType.DMA((3 + 2 * chunks, 6)),
            pltpu.SemaphoreType.DMA((3 + 2 * chunks, 6)),
        ],
        compiler_params=pltpu.CompilerParams(
            collective_id=1, has_side_effects=True, vmem_limit_bytes=48 << 20
        ),
        name="reduce_error",
    )(weight, chosen, coeffs, mask, limit, features)


def local(weight, hess_inv, selected, block_mask, row_limits, calibration):
    rows_local, cols_local = hess_inv.shape
    out_local = weight.shape[0]
    row_offset = lax.axis_index("rows") * rows_local
    chosen = selected.reshape(-1)
    count = chosen.shape[0]
    row_place = chosen - row_offset
    row_inside = (row_place >= 0) & (row_place < rows_local)
    own_rows = jnp.where(
        row_inside[:, None],
        jnp.take(hess_inv, jnp.clip(row_place, 0, rows_local - 1), axis=0),
        0.0,
    )
    line = jnp.broadcast_to(jnp.pad(chosen, (0, LANES - count), constant_values=-1)[None, :], (8, LANES))
    square, panel, weight_cols = exchange(own_rows, weight, line)
    coeffs = solve(square, panel)
    limit = jnp.broadcast_to(row_limits[None, :], (16, out_local)).astype(jnp.bfloat16)
    pruned, error = reduce_error(weight, weight_cols, coeffs, block_mask, limit, calibration)
    return (pruned, error.T)


def solution(mesh):
    placed = (
        P("rows", "cols"),
        P("rows", "cols"),
        P(),
        P("rows", None),
        P("rows"),
        P(None, "cols"),
    )
    return jax.shard_map(
        local,
        mesh=mesh,
        in_specs=placed,
        out_specs=(P("rows", "cols"), P("rows", "cols")),
        check_vma=False,
    )
```

```python
import functools

import jax
import jax.numpy as jnp
from jax import lax
from jax.experimental import pallas as pl
from jax.experimental.pallas import tpu as pltpu
from jax.sharding import PartitionSpec as P

BLK = 128
LANES = 256
MESH = pl.DeviceIdType.MESH
HIGHEST = lax.Precision.HIGHEST


def aligned(value, factor):
    return pl.multiple_of(value, factor)


def place():
    row = lax.axis_index("rows")
    col = lax.axis_index("cols")
    core = lax.rem(col, 2)
    z = lax.rem(col // 2, 4)
    y = col // 8
    partner = (row, col + 1 - 2 * core)
    axes = {
        "x": (row, lambda j: (j, col)),
        "y": (y, lambda j: (row, (j * 4 + z) * 2 + core)),
        "z": (z, lambda j: (row, (y * 4 + j) * 2 + core)),
    }
    return core, partner, axes


def enter(partner, axes):
    barrier = pltpu.get_barrier_semaphore()
    pl.semaphore_signal(barrier, inc=1, device_id=partner, device_id_type=MESH)
    for index, device in axes.values():
        for step in (1, 2, 3):
            pl.semaphore_signal(
                barrier, inc=1, device_id=device(lax.rem(index + step, 4)), device_id_type=MESH
            )
    pl.semaphore_wait(barrier, 1 + 3 * len(axes))


def exchange_kernel(
    own_ref, weight_ref, line_ref, square_ref, panel_ref, chosen_ref,
    square_part, half_rx, half, z_rx, z_sum, y_rx, y_sum, x_rx,
    panel_rx, weight_part, weight_rx, weight_half, first_rx, first_sum, second_rx,
    send_sem, recv_sem,
):
    core, partner, axes = place()
    col_offset = lax.axis_index("cols") * weight_ref.shape[1]
    count = own_ref.shape[0]
    half_rows = count // 2
    quarter = half_rows // 4
    started = []

    def send(src, dst, stage, slot, device):
        copy = pltpu.make_async_remote_copy(
            src_ref=src, dst_ref=dst, send_sem=send_sem.at[stage, slot], recv_sem=recv_sem.at[stage, slot],
            device_id=device, device_id_type=MESH,
        )
        copy.start()
        started.append(copy)
        return copy

    def scatter(axis, src, base, piece, rx, stage):
        index, device = axes[axis]
        copies = []
        for step in (1, 2, 3):
            peer = lax.rem(index + step, 4)
            start = aligned(base + peer * piece, 8)
            copies.append(send(src.at[pl.ds(start, piece)], rx.at[step - 1], stage, step - 1, device(peer)))
        return copies

    def spread(axis, src, dst_of, stage):
        index, device = axes[axis]
        return [
            send(src, dst_of(step - 1), stage, step - 1, device(lax.rem(index + step, 4))) for step in (1, 2, 3)
        ]

    def arrive(copies):
        for copy in copies:
            copy.wait_recv()

    def total(own, rx):
        return own + rx[0] + rx[1] + rx[2]

    enter(partner, axes)

    x, y, z = axes["x"][0], axes["y"][0], axes["z"][0]
    lines = lax.broadcasted_iota(jnp.int32, (weight_ref.shape[1], LANES), 0) + col_offset
    onehot = jnp.where(lines == line_ref[0:1, :], 1.0, 0.0)
    square_part[...] = jnp.dot(own_ref[...], onehot, precision=HIGHEST, preferred_element_type=jnp.float32)
    s1 = send(
        square_part.at[pl.ds(aligned((1 - core) * half_rows, 8), half_rows)], half_rx, 0, 0, partner
    )
    panel_piece = count // 4
    p1 = scatter("x", own_ref, 0, panel_piece, panel_rx, 1)
    weight_part[...] = jnp.dot(
        weight_ref[...], onehot.astype(jnp.bfloat16), preferred_element_type=jnp.float32
    ).astype(jnp.bfloat16)
    rows = weight_ref.shape[0]
    share = rows // 2
    w1 = send(weight_part.at[pl.ds(aligned((1 - core) * share, 16), share)], weight_rx, 2, 0, partner)
    s1.wait_recv()
    half[...] = square_part[pl.ds(aligned(core * half_rows, 8), half_rows), :] + half_rx[...]
    s2 = scatter("z", half, 0, quarter, z_rx, 3)
    arrive(s2)
    z_sum[...] = total(half[pl.ds(aligned(z * quarter, 8), quarter), :], z_rx)
    s3 = spread("y", z_sum, lambda slot: y_rx.at[slot], 4)
    w1.wait_recv()
    weight_half[...] = weight_part[pl.ds(aligned(core * share, 16), share), :] + weight_rx[...]
    arrive(s3)
    y_sum[...] = total(z_sum[...], y_rx)
    s4 = spread("x", y_sum, lambda slot: x_rx.at[slot], 5)
    part = share // 2
    piece = part // 4
    small = piece // 4
    wa = scatter("y", weight_half, 0, piece, first_rx.at[0], 6)
    wb = scatter("z", weight_half, part, piece, first_rx.at[1], 7)
    arrive(s4)
    mine = pl.ds(aligned(core * half_rows + z * quarter, 8), quarter)
    square_ref[mine, :] = total(y_sum[...], x_rx)
    s5 = spread("z", square_ref.at[mine], lambda slot: square_ref.at[mine], 8)
    arrive(p1)
    own_panel = pl.ds(aligned(x * panel_piece, 8), panel_piece)
    panel_ref[own_panel, :] = total(own_ref[own_panel, :], panel_rx)
    p2 = spread("x", panel_ref.at[own_panel], lambda slot: panel_ref.at[own_panel], 9)
    arrive(s5)
    own_half = pl.ds(aligned(core * half_rows, 8), half_rows)
    s6 = send(square_ref.at[own_half], square_ref.at[own_half], 10, 0, partner)
    arrive(wa)
    first_sum[0] = total(weight_half[pl.ds(aligned(y * piece, 16), piece), :], first_rx.at[0])
    wa = scatter("z", first_sum.at[0], 0, small, second_rx.at[0], 11)
    arrive(wb)
    first_sum[1] = total(weight_half[pl.ds(aligned(part + z * piece, 16), piece), :], first_rx.at[1])
    wb = scatter("y", first_sum.at[1], 0, small, second_rx.at[1], 12)
    arrive(wa)
    base_a = core * share + y * piece
    base_b = core * share + part + z * piece
    slice_a = pl.ds(aligned(base_a + z * small, 16), small)
    slice_b = pl.ds(aligned(base_b + y * small, 16), small)
    chosen_ref[slice_a, :] = total(first_sum[0, pl.ds(aligned(z * small, 16), small), :], second_rx.at[0])
    wa = spread("z", chosen_ref.at[slice_a], lambda slot: chosen_ref.at[slice_a], 13)
    arrive(wb)
    chosen_ref[slice_b, :] = total(first_sum[1, pl.ds(aligned(y * small, 16), small), :], second_rx.at[1])
    wb = spread("y", chosen_ref.at[slice_b], lambda slot: chosen_ref.at[slice_b], 14)
    arrive(wa)
    piece_a = pl.ds(aligned(base_a, 16), piece)
    wa = spread("y", chosen_ref.at[piece_a], lambda slot: chosen_ref.at[piece_a], 15)
    arrive(wb)
    piece_b = pl.ds(aligned(base_b, 16), piece)
    wb = spread("z", chosen_ref.at[piece_b], lambda slot: chosen_ref.at[piece_b], 16)
    arrive(wa)
    arrive(wb)
    own_share = pl.ds(aligned(core * share, 16), share)
    w6 = send(chosen_ref.at[own_share], chosen_ref.at[own_share], 17, 0, partner)
    arrive(p2)
    s6.wait_recv()
    w6.wait_recv()
    for copy in started:
        copy.wait_send()


def exchange(own_rows, weight, line):
    count, columns = own_rows.shape
    rows = weight.shape[0]
    f32, bf16 = jnp.float32, jnp.bfloat16
    half, quarter = count // 2, count // 8
    share = rows // 2
    piece = share // 8
    small = piece // 4
    vmem = pl.BlockSpec(memory_space=pltpu.VMEM)
    return pl.pallas_call(
        exchange_kernel,
        out_shape=(
            jax.ShapeDtypeStruct((count, LANES), f32),
            jax.ShapeDtypeStruct((count, columns), f32),
            jax.ShapeDtypeStruct((rows, LANES), bf16),
        ),
        in_specs=[vmem] * 3,
        out_specs=(vmem,) * 3,
        scratch_shapes=[
            pltpu.VMEM((count, LANES), f32),
            pltpu.VMEM((half, LANES), f32),
            pltpu.VMEM((half, LANES), f32),
            pltpu.VMEM((3, quarter, LANES), f32),
            pltpu.VMEM((quarter, LANES), f32),
            pltpu.VMEM((3, quarter, LANES), f32),
            pltpu.VMEM((quarter, LANES), f32),
            pltpu.VMEM((3, quarter, LANES), f32),
            pltpu.VMEM((3, count // 4, columns), f32),
            pltpu.VMEM((rows, LANES), bf16),
            pltpu.VMEM((share, LANES), bf16),
            pltpu.VMEM((share, LANES), bf16),
            pltpu.VMEM((2, 3, piece, LANES), bf16),
            pltpu.VMEM((2, piece, LANES), bf16),
            pltpu.VMEM((2, 3, small, LANES), bf16),
            pltpu.SemaphoreType.DMA((18, 3)),
            pltpu.SemaphoreType.DMA((18, 3)),
        ],
        compiler_params=pltpu.CompilerParams(
            collective_id=0, has_side_effects=True, vmem_limit_bytes=40 << 20
        ),
        name="exchange",
    )(own_rows, weight, line)


def gather_kernel(offset_ref, selected_ref, inverse_ref, own_ref, line_ref, sems):
    steps, width = selected_ref.shape
    height = inverse_ref.shape[0]
    lane = lax.broadcasted_iota(jnp.int32, line_ref.shape, 1)

    def wanted(k):
        return selected_ref[k // width, lax.rem(k, width)]

    def row_copy(k, spot):
        return pltpu.make_async_copy(inverse_ref.at[pl.ds(spot, 1)], own_ref.at[pl.ds(k, 1)], sems.at[k])

    def start(k, line):
        picked = wanted(k)
        spot = picked - offset_ref[0]
        inside = (spot >= 0) & (spot < height)

        @pl.when(inside)
        def _():
            row_copy(k, spot).start()

        @pl.when(jnp.logical_not(inside))
        def _():
            own_ref[pl.ds(k, 1), :] = jnp.zeros((1, own_ref.shape[1]), jnp.float32)

        return jnp.where(lane == k, picked, line)

    line_ref[...] = lax.fori_loop(0, steps * width, start, jnp.full(line_ref.shape, -1, jnp.int32))

    def finish(k, carry):
        spot = wanted(k) - offset_ref[0]

        @pl.when((spot >= 0) & (spot < height))
        def _():
            row_copy(k, spot).wait()

        return carry

    lax.fori_loop(0, steps * width, finish, 0)


def gather(offset, selected, inverse):
    count = selected.size
    smem = pl.BlockSpec(memory_space=pltpu.SMEM)
    vmem = pl.BlockSpec(memory_space=pltpu.VMEM)
    return pl.pallas_call(
        gather_kernel,
        out_shape=(
            jax.ShapeDtypeStruct((count, inverse.shape[1]), jnp.float32),
            jax.ShapeDtypeStruct((8, LANES), jnp.int32),
        ),
        in_specs=[smem, smem, pl.BlockSpec(memory_space=pl.ANY)],
        out_specs=(vmem, vmem),
        scratch_shapes=[pltpu.SemaphoreType.DMA((count,))],
        name="gather",
    )(offset, selected, inverse)


def invert(state):
    count = state.shape[0]
    size = 8
    lane = lax.broadcasted_iota(jnp.int32, (size, BLK), 1)
    line = lax.broadcasted_iota(jnp.int32, (size, BLK), 0)

    def column(tile, at):
        return jnp.take_along_axis(tile, jnp.full((size, BLK), at, jnp.int32), axis=1)

    def row(tile, k):
        return jnp.broadcast_to(tile[k : k + 1, :], tile.shape)

    def lines_of(block):
        return pl.ds(aligned(block * size, size), size)

    def spot_of(block):
        half = block * size // BLK
        return half, block * size - half * BLK

    def tile_of(half):
        return pl.ds(aligned(half * BLK, BLK), BLK)

    def blend(tile, columns, rows):
        for j in range(0, size, 2):
            tile = tile - (columns[j] * rows[j] + columns[j + 1] * rows[j + 1])
        return tile

    def columns_of(tile, at):
        return [column(tile, at + j) for j in range(size)]

    def step(block, pivot):
        pivot = list(pivot)
        for k in range(size):
            scale = 1.0 / row(pivot[k], k)
            lead = pivot[k]
            for j in range(size):
                if j != k:
                    scaled = row(pivot[j], k) * scale
                    pivot[j] = jnp.where(line == k, scaled, pivot[j] - lead * scaled)
            pivot[k] = jnp.where(line == k, scale, -lead * scale)
        half, at = spot_of(block)
        inside = (lane >= at) & (lane < at + size)
        unit = jnp.where(lane - at == line, 1.0, 0.0)
        fresh, rows, here = [], [], []
        for q in range(state.shape[1] // BLK):
            mine = inside & (half == q)
            here.append(mine)
            tile = jnp.where(mine, unit, state[lines_of(block), q * BLK : (q + 1) * BLK])
            parts = [pivot[j] * row(tile, j) for j in range(size)]
            while len(parts) > 1:
                parts = [parts[i] + parts[i + 1] for i in range(0, len(parts), 2)]
            fresh.append(parts[0])
            rows.append([row(parts[0], j) for j in range(size)])
        following = jnp.minimum(block + 1, count // size - 1)
        next_half, next_at = spot_of(following)
        ahead = columns_of(state[lines_of(following), tile_of(half)], at)
        next_fresh = jnp.where(next_half == 0, fresh[0], fresh[1])
        next_tile = jnp.where(inside & (half == next_half), 0.0, state[lines_of(following), tile_of(next_half)])
        next_tile = blend(next_tile, ahead, [row(next_fresh, j) for j in range(size)])
        next_pivot = columns_of(next_tile, next_at)
        for i in range(count // size):
            group = slice(i * size, (i + 1) * size)
            columns = columns_of(state[group, tile_of(half)], at)
            for q in range(state.shape[1] // BLK):
                lanes = slice(q * BLK, (q + 1) * BLK)
                tile = jnp.where(here[q], 0.0, state[group, lanes])
                state[group, lanes] = blend(tile, columns, rows[q])
        for q in range(state.shape[1] // BLK):
            state[lines_of(block), q * BLK : (q + 1) * BLK] = fresh[q]
        return tuple(next_pivot)

    first = tuple(columns_of(state[0:size, 0:BLK], 0))
    return step, first


def invert_kernel(square_ref, panel_ref, coeffs_ref, state):
    count = square_ref.shape[0]
    state[...] = square_ref[...]
    step, first = invert(state)
    lax.fori_loop(0, count // 8, step, first)
    coeffs_ref[...] = jnp.dot(
        state[:, :count], panel_ref[...], precision=HIGHEST, preferred_element_type=jnp.float32
    )


def solve(square, panel):
    return pl.pallas_call(
        invert_kernel,
        out_shape=jax.ShapeDtypeStruct(panel.shape, jnp.float32),
        in_specs=[pl.BlockSpec(memory_space=pltpu.VMEM)] * 2,
        out_specs=pl.BlockSpec(memory_space=pltpu.VMEM),
        scratch_shapes=[pltpu.VMEM(square.shape, jnp.float32)],
        name="solve",
    )(square, panel)


def reduce_kernel(
    weight_ref, chosen_ref, coeffs_ref, mask_ref, limit_ref, features_ref, pruned_ref, error_ref,
    high, low, features_rx, own_diff, sent_diff, diff_rx, part, forward_rx, forward, ring_rx,
    sums, sums_wide, small_forward_rx, small_forward, small_rx, final,
    send_sem, recv_sem,
):
    core, partner, axes = place()
    axes = {name: axes[name] for name in ("y", "z")}
    rows, columns = weight_ref.shape
    share = rows // 2
    chunks = part.shape[0]
    chunk = share // chunks
    blocks = columns // BLK
    tokens_axis = part.shape[1]
    first_block = lax.axis_index("cols") * blocks
    started = []

    def remote(src, dst, stage, slot, device):
        return pltpu.make_async_remote_copy(
            src_ref=src, dst_ref=dst, send_sem=send_sem.at[stage, slot], recv_sem=recv_sem.at[stage, slot],
            device_id=device, device_id_type=MESH,
        )

    def send(*args):
        copy = remote(*args)
        copy.start()
        started.append(copy)
        return copy

    enter(partner, axes)
    features_copy = send(features_ref, features_rx, 0, 0, partner)

    coeffs = coeffs_ref[...]
    high[...] = coeffs.astype(jnp.bfloat16)
    low[...] = (coeffs - high[...].astype(jnp.float32)).astype(jnp.bfloat16)
    count = coeffs_ref.shape[0]
    line = lax.broadcasted_iota(jnp.int32, (BLK, columns), 0)
    block = first_block + lax.broadcasted_iota(jnp.int32, (BLK, columns), 1) // BLK
    before = jnp.where(line <= block, 1.0, 0.0).astype(jnp.bfloat16)
    here = jnp.where(line == block, 1.0, 0.0).astype(jnp.bfloat16)
    spread = jnp.where(lax.broadcasted_iota(jnp.int32, (16, columns), 0) == 0, 1.0, 0.0).astype(jnp.bfloat16)

    def differ(first, store):
        lines = pl.ds(aligned(first, chunk), chunk)
        picked = chosen_ref[lines, :][:, :count]
        change = jnp.dot(picked, high[...], preferred_element_type=jnp.float32)
        change += jnp.dot(picked, low[...], preferred_element_type=jnp.float32)
        mask = mask_ref[lines, :].astype(jnp.float32).astype(jnp.bfloat16)
        seen = jnp.dot(mask, before, preferred_element_type=jnp.float32)
        bit = jnp.dot(mask, here, preferred_element_type=jnp.float32)
        limit = lax.dot_general(
            limit_ref[:, lines], spread, (((0,), (0,)), ((), ())), preferred_element_type=jnp.float32
        )
        kept = jnp.where(seen <= limit, bit, 0.0)
        wide = weight_ref[lines, :].astype(jnp.float32)
        masked = (wide - change) * kept
        pruned_ref[lines, :] = masked.astype(jnp.bfloat16)
        store((wide - masked).astype(jnp.bfloat16))

    def diff_copy(i):
        lines = pl.ds(aligned(i * chunk, chunk), chunk)
        return remote(sent_diff.at[lines], diff_rx.at[lines], 1, i, partner)

    @pl.loop(0, chunks)
    def _(i):
        def store(value):
            sent_diff[pl.ds(aligned(i * chunk, chunk), chunk), :] = value

        differ((1 - core) * share + i * chunk, store)
        diff_copy(i).start()

    @pl.loop(0, chunks)
    def _(i):
        def store(value):
            own_diff[pl.ds(aligned(i * chunk, chunk), chunk), :] = value

        differ(core * share + i * chunk, store)

    features_copy.wait_recv()

    def multiply(k):
        lines = pl.ds(k * chunk, chunk)
        tokens = features_ref.shape[0] // tokens_axis

        @pl.loop(0, tokens_axis)
        def _(t):
            words = pl.ds(aligned(t * tokens, tokens), tokens)
            product = lax.dot_general(
                features_ref[words, :], own_diff[lines, :], (((1,), (1,)), ((), ())),
                preferred_element_type=jnp.float32,
            )
            product += lax.dot_general(
                features_rx[words, :], diff_rx[lines, :], (((1,), (1,)), ((), ())),
                preferred_element_type=jnp.float32,
            )
            part[k, t] = product.astype(jnp.bfloat16).reshape(part.shape[2:])

    def ring(axis, sent, value, extent, through_rx, through, rx, stage):
        index, device = axes[axis]
        right, left, across = lax.rem(index + 1, 4), lax.rem(index + 3, 4), lax.rem(index + 2, 4)
        lo, hi = pl.ds(0, extent // 2), pl.ds(extent // 2, extent // 2)
        a = send(sent(across).at[lo], through_rx.at[0], stage, 0, device(right))
        b = send(sent(across).at[hi], through_rx.at[1], stage, 1, device(left))
        c = send(sent(right).at[hi], rx.at[0, hi], stage, 2, device(right))
        d = send(sent(left).at[lo], rx.at[1, lo], stage, 3, device(left))
        later = []

        def pass_on():
            a.wait_recv()
            through[0] = (value(right, lo) + through_rx[0].astype(jnp.float32)).astype(jnp.bfloat16)
            later.append(send(through.at[0], rx.at[0, lo], stage, 4, device(right)))
            b.wait_recv()
            through[1] = (value(left, hi) + through_rx[1].astype(jnp.float32)).astype(jnp.bfloat16)
            later.append(send(through.at[1], rx.at[1, hi], stage, 5, device(left)))

        def finish():
            for copy in (c, d, *later):
                copy.wait_recv()
            return value(index, pl.ds(0, extent)) + rx[0].astype(jnp.float32) + rx[1].astype(jnp.float32)

        return pass_on, finish

    order = [k for pair in zip(range(chunks // 2), range(chunks // 2, chunks)) for k in pair]
    rings = {}
    for k in order:
        diff_copy(k).wait_recv()
        multiply(k)
        if k < chunks // 2:
            axis = "y"
            sent = functools.partial(lambda k, j: part.at[k, j], k)
        else:
            axis = "z"
            sent = functools.partial(lambda k, j: part.at[k, :, j], k)
        value = functools.partial(lambda sent, j, which: sent(j).at[which][...].astype(jnp.float32), sent)
        rings[k] = ring(axis, sent, value, 4, forward_rx.at[k], forward.at[k], ring_rx.at[k], 2 + k)
    for k in order:
        rings[k][0]()
    again = {}
    for k in order:
        total = rings[k][1]()
        sums_wide[k] = total
        sums[k] = total.astype(jnp.bfloat16)
        axis = "z" if k < chunks // 2 else "y"
        sent = functools.partial(lambda k, j: sums.at[k, j], k)
        value = functools.partial(lambda k, j, which: sums_wide[k, j, which, :], k)
        again[k] = ring(
            axis, sent, value, 64, small_forward_rx.at[k], small_forward.at[k], small_rx.at[k], 2 + chunks + k
        )
    for k in order:
        again[k][0]()
    tokens = error_ref.shape[0]
    last = []
    for k in order:
        final[k] = again[k][1]()
        lanes = pl.ds(aligned(core * share + k * chunk, chunk), chunk)
        last.append(
            send(
                final.at[k, pl.ds(aligned((1 - core) * tokens, tokens), tokens)],
                error_ref.at[:, lanes], 2 + 2 * chunks, k, partner,
            )
        )
        error_ref[:, lanes] = final[k, pl.ds(aligned(core * tokens, tokens), tokens), :]
    for copy in last:
        copy.wait_recv()
    for i in range(chunks):
        diff_copy(i).wait_send()
    for copy in started:
        copy.wait_send()


def reduce_error(weight, chosen, coeffs, mask, limit, features):
    rows, columns = weight.shape
    tokens = features.shape[0]
    f32, bf16 = jnp.float32, jnp.bfloat16
    share, chunks = rows // 2, 4
    chunk = share // chunks
    vmem = pl.BlockSpec(memory_space=pltpu.VMEM)
    return pl.pallas_call(
        reduce_kernel,
        out_shape=(
            jax.ShapeDtypeStruct((rows, columns), bf16),
            jax.ShapeDtypeStruct((tokens // 32, rows), f32),
        ),
        in_specs=[vmem] * 6,
        out_specs=(vmem,) * 2,
        scratch_shapes=[
            pltpu.VMEM(coeffs.shape, bf16),
            pltpu.VMEM(coeffs.shape, bf16),
            pltpu.VMEM(features.shape, bf16),
            pltpu.VMEM((share, columns), bf16),
            pltpu.VMEM((share, columns), bf16),
            pltpu.VMEM((share, columns), bf16),
            pltpu.VMEM((chunks, 4, 4, 64, chunk), bf16),
            pltpu.VMEM((chunks, 2, 2, 64, chunk), bf16),
            pltpu.VMEM((chunks, 2, 2, 64, chunk), bf16),
            pltpu.VMEM((chunks, 2, 4, 64, chunk), bf16),
            pltpu.VMEM((chunks, 4, 64, chunk), bf16),
            pltpu.VMEM((chunks, 4, 64, chunk), f32),
            pltpu.VMEM((chunks, 2, 32, chunk), bf16),
            pltpu.VMEM((chunks, 2, 32, chunk), bf16),
            pltpu.VMEM((chunks, 2, 64, chunk), bf16),
            pltpu.VMEM((chunks, 64, chunk), f32),
            pltpu.SemaphoreType.DMA((3 + 2 * chunks, 6)),
            pltpu.SemaphoreType.DMA((3 + 2 * chunks, 6)),
        ],
        compiler_params=pltpu.CompilerParams(
            collective_id=1, has_side_effects=True, vmem_limit_bytes=48 << 20
        ),
        name="reduce_error",
    )(weight, chosen, coeffs, mask, limit, features)


def local(weight, hess_inv, selected, block_mask, row_limits, calibration):
    rows_local = hess_inv.shape[0]
    out_local = weight.shape[0]
    row_offset = (lax.axis_index("rows") * rows_local).astype(jnp.int32).reshape(1)
    own_rows, line = gather(row_offset, selected, hess_inv)
    square, panel, weight_cols = exchange(own_rows, weight, line)
    coeffs = solve(square, panel)
    limit = jnp.broadcast_to(row_limits[None, :], (16, out_local)).astype(jnp.bfloat16)
    pruned, error = reduce_error(weight, weight_cols, coeffs, block_mask, limit, calibration)
    return (pruned, error.T)


def solution(mesh):
    placed = (
        P("rows", "cols"),
        P("rows", "cols"),
        P(),
        P("rows", None),
        P("rows"),
        P(None, "cols"),
    )
    return jax.shard_map(
        local,
        mesh=mesh,
        in_specs=placed,
        out_specs=(P("rows", "cols"), P("rows", "cols")),
        check_vma=False,
    )
```

```python
import functools

import jax
import jax.numpy as jnp
from jax import lax
from jax.experimental import pallas as pl
from jax.experimental.pallas import tpu as pltpu
from jax.sharding import PartitionSpec as P

BLK = 128
LANES = 256
MESH = pl.DeviceIdType.MESH
HIGHEST = lax.Precision.HIGHEST


def aligned(value, factor):
    return pl.multiple_of(value, factor)


def place():
    row = lax.axis_index("rows")
    col = lax.axis_index("cols")
    core = lax.rem(col, 2)
    z = lax.rem(col // 2, 4)
    y = col // 8
    partner = (row, col + 1 - 2 * core)
    axes = {
        "x": (row, lambda j: (j, col)),
        "y": (y, lambda j: (row, (j * 4 + z) * 2 + core)),
        "z": (z, lambda j: (row, (y * 4 + j) * 2 + core)),
    }
    return core, partner, axes


def enter(partner, axes):
    barrier = pltpu.get_barrier_semaphore()
    pl.semaphore_signal(barrier, inc=1, device_id=partner, device_id_type=MESH)
    for index, device in axes.values():
        for step in (1, 2, 3):
            pl.semaphore_signal(
                barrier, inc=1, device_id=device(lax.rem(index + step, 4)), device_id_type=MESH
            )
    pl.semaphore_wait(barrier, 1 + 3 * len(axes))


def gather_kernel(offset_ref, selected_ref, values_ref, inverse_ref, own_ref, line_ref, sem):
    steps, width = selected_ref.shape
    height = inverse_ref.shape[0]
    for step in range(steps):

        @pl.loop(0, width, unroll=16)
        def _(k):
            spot = jnp.clip(selected_ref[step, k] - offset_ref[0], 0, height - 1)
            pltpu.make_async_copy(
                inverse_ref.at[pl.ds(spot, 1)], own_ref.at[pl.ds(step * width + k, 1)], sem
            ).start()

    line_ref[...] = jnp.full(line_ref.shape, -1, jnp.int32)
    for step in range(steps):
        line_ref[0:1, step * width : (step + 1) * width] = values_ref[step : step + 1, :]
    pltpu.make_async_copy(inverse_ref.at[pl.ds(0, own_ref.shape[0])], own_ref, sem).wait()


def gather(offset, selected, inverse):
    count = selected.size
    smem = pl.BlockSpec(memory_space=pltpu.SMEM)
    vmem = pl.BlockSpec(memory_space=pltpu.VMEM)
    return pl.pallas_call(
        gather_kernel,
        out_shape=(
            jax.ShapeDtypeStruct((count, inverse.shape[1]), jnp.float32),
            jax.ShapeDtypeStruct((8, LANES), jnp.int32),
        ),
        in_specs=[smem, smem, vmem, pl.BlockSpec(memory_space=pl.ANY)],
        out_specs=(vmem, vmem),
        scratch_shapes=[pltpu.SemaphoreType.DMA],
        name="gather",
    )(offset, selected, selected, inverse)


def invert(state, right, between):
    count, width = state.shape
    size, side = 8, 64
    blocks = side // size
    lane = lax.broadcasted_iota(jnp.int32, (size, BLK), 1)
    line = lax.broadcasted_iota(jnp.int32, (size, BLK), 0)

    def column(tile, at):
        return jnp.take_along_axis(tile, jnp.full((size, BLK), at, jnp.int32), axis=1)

    def row(tile, k):
        return jnp.broadcast_to(tile[k : k + 1, :], tile.shape)

    def fold(parts):
        while len(parts) > 1:
            parts = [parts[i] + parts[i + 1] for i in range(0, len(parts), 2)]
        return parts[0]

    def step(t, carry):
        half = t // 2
        shift = (t - half * 2) * side
        lanes = pl.ds(aligned(half * BLK, BLK), BLK)
        groups = [state[pl.ds(aligned(t * side + i * size, size), size), lanes] for i in range(blocks)]
        for b in range(blocks):
            at = shift + b * size
            pivot = [column(groups[b], at + j) for j in range(size)]
            for k in range(size):
                scale = 1.0 / row(pivot[k], k)
                lead = pivot[k]
                for j in range(size):
                    if j != k:
                        scaled = row(pivot[j], k) * scale
                        pivot[j] = jnp.where(line == k, scaled, pivot[j] - lead * scaled)
                pivot[k] = jnp.where(line == k, scale, -lead * scale)
            inside = (lane >= at) & (lane < at + size)
            tile = jnp.where(inside, jnp.where(lane - at == line, 1.0, 0.0), groups[b])
            fresh = fold([pivot[j] * row(tile, j) for j in range(size)])
            rows = [row(fresh, j) for j in range(size)]
            order = [(b + 1 + i) % blocks for i in range(blocks - 1)]
            for i in order:
                change = fold([column(groups[i], at + j) * rows[j] for j in range(size)])
                groups[i] = jnp.where(inside, 0.0, groups[i]) - change
            groups[b] = fresh
        mine = (lane >= shift) & (lane < shift + side)
        block = jnp.concatenate([jnp.where(mine, group, 0.0) for group in groups], axis=0)
        own = pl.ds(aligned(shift, side), side)
        lines = pl.ds(aligned(t * side, side), side)
        wide = lax.broadcasted_iota(jnp.int32, (side, width), 1) - t * side
        unit = jnp.where(wide == lax.broadcasted_iota(jnp.int32, (side, width), 0), 1.0, 0.0)
        right[...] = jnp.zeros(right.shape, jnp.float32)
        right[own, :] = jnp.where((wide >= 0) & (wide < side), unit, state[lines, :])
        solved = jnp.dot(block, right[...], precision=HIGHEST, preferred_element_type=jnp.float32)
        right[own, :] = solved
        tall = lax.broadcasted_iota(jnp.int32, (count, BLK), 1)
        strip = jnp.where((tall >= shift) & (tall < shift + side), state[:, lanes], 0.0)
        spans = lax.broadcasted_iota(jnp.int32, (count, width), 1) - t * side
        cleared = jnp.where((spans >= 0) & (spans < side), 0.0, state[...])
        state[...] = cleared - jnp.dot(strip, right[...], precision=HIGHEST, preferred_element_type=jnp.float32)
        state[lines, :] = solved
        between(t)
        return carry

    lax.fori_loop(0, count // side, step, 0)


def prune_kernel(
    own_ref, line_ref, limit_ref, weight_any, mask_any, features_any, pruned_any, error_ref,
    weight_ref, mask_ref, features_ref, kept, limits,
    own_rows, square_part, half_rx, half, z_rx, z_sum, y_rx, y_sum, x_rx, square_ref, state, right,
    panel_rx, panel_ref, weight_part, weight_rx, weight_half, first_rx, first_sum, second_rx, chosen_ref,
    high, low, features_rx, own_diff, sent_diff, diff_rx, pruned_ref, part, forward_rx, forward, ring_rx,
    sums, sums_wide, small_forward_rx, small_forward, small_rx, final,
    send_sem, recv_sem, local_sem, pruned_sem,
    *, height,
):
    core, partner, axes = place()
    rows, columns = weight_ref.shape
    col_offset = lax.axis_index("cols") * columns
    count = own_ref.shape[0]
    half_rows = count // 2
    quarter = half_rows // 4
    share = rows // 2
    chunks = part.shape[0]
    chunk = share // chunks
    blocks = columns // BLK
    f32, bf16 = jnp.float32, jnp.bfloat16
    started = []

    loads = [
        pltpu.make_async_copy(src, dst, local_sem.at[i])
        for i, (src, dst) in enumerate(
            ((weight_any, weight_ref), (features_any, features_ref), (mask_any, mask_ref))
        )
    ]
    for load in loads:
        load.start()

    def remote(src, dst, stage, slot, device):
        return pltpu.make_async_remote_copy(
            src_ref=src, dst_ref=dst, send_sem=send_sem.at[stage, slot], recv_sem=recv_sem.at[stage, slot],
            device_id=device, device_id_type=MESH,
        )

    def send(*args):
        copy = remote(*args)
        copy.start()
        started.append(copy)
        return copy

    def scatter(axis, src, base, piece, rx, stage):
        index, device = axes[axis]
        copies = []
        for step in (1, 2, 3):
            peer = lax.rem(index + step, 4)
            start = aligned(base + peer * piece, 8)
            copies.append(send(src.at[pl.ds(start, piece)], rx.at[step - 1], stage, step - 1, device(peer)))
        return copies

    def spread(axis, src, dst_of, stage):
        index, device = axes[axis]
        return [
            send(src, dst_of(step - 1), stage, step - 1, device(lax.rem(index + step, 4))) for step in (1, 2, 3)
        ]

    def arrive(copies):
        for copy in copies:
            copy.wait_recv()

    def total(own, rx):
        return own + rx[0] + rx[1] + rx[2]

    row_offset = lax.axis_index("rows") * height
    picked = line_ref[0:1, :count]
    owned = jnp.where((picked >= row_offset) & (picked < row_offset + height), 1.0, 0.0)
    first = lax.broadcasted_iota(jnp.int32, (16, count), 0) == 0
    owned = lax.dot_general(
        jnp.where(first, owned, 0.0).astype(bf16), jnp.ones((16, columns), bf16),
        (((0,), (0,)), ((), ())), preferred_element_type=f32,
    )
    own_rows[...] = jnp.where(owned > 0.5, own_ref[...], 0.0)
    lines = lax.broadcasted_iota(jnp.int32, (columns, LANES), 0) + col_offset
    onehot = jnp.where(lines == line_ref[0:1, :], 1.0, 0.0)
    square_part[...] = jnp.dot(own_rows[...], onehot, precision=HIGHEST, preferred_element_type=f32)
    loads[0].wait()
    weight_part[...] = jnp.dot(weight_ref[...], onehot.astype(bf16), preferred_element_type=f32).astype(bf16)

    enter(partner, axes)
    x, y, z = axes["x"][0], axes["y"][0], axes["z"][0]
    s1 = send(square_part.at[pl.ds(aligned((1 - core) * half_rows, 8), half_rows)], half_rx, 0, 0, partner)
    w1 = send(weight_part.at[pl.ds(aligned((1 - core) * share, 16), share)], weight_rx, 2, 0, partner)
    panel_piece = count // 4
    p1 = scatter("x", own_rows, 0, panel_piece, panel_rx, 1)
    loads[1].wait()
    features_copy = send(features_ref, features_rx, 18, 0, partner)
    s1.wait_recv()
    half[...] = square_part[pl.ds(aligned(core * half_rows, 8), half_rows), :] + half_rx[...]
    s2 = scatter("z", half, 0, quarter, z_rx, 3)
    w1.wait_recv()
    weight_half[...] = weight_part[pl.ds(aligned(core * share, 16), share), :] + weight_rx[...]
    span = share // 2
    piece = span // 4
    small = piece // 4
    wa = scatter("y", weight_half, 0, piece, first_rx.at[0], 6)
    wb = scatter("z", weight_half, span, piece, first_rx.at[1], 7)

    loads[2].wait()
    limits[...] = jnp.broadcast_to(limit_ref[0:1, :].astype(f32), limits.shape).astype(bf16)
    place_line = lax.broadcasted_iota(jnp.int32, (BLK, columns), 0)
    block = lax.axis_index("cols") * blocks + lax.broadcasted_iota(jnp.int32, (BLK, columns), 1) // BLK
    before = jnp.where(place_line <= block, 1.0, 0.0).astype(bf16)
    here = jnp.where(place_line == block, 1.0, 0.0).astype(bf16)
    lead = jnp.where(lax.broadcasted_iota(jnp.int32, (16, columns), 0) == 0, 1.0, 0.0).astype(bf16)

    def keep(low_chunk, high_chunk):
        @pl.loop(low_chunk, high_chunk)
        def _(i):
            spots = pl.ds(aligned(i * chunk, chunk), chunk)
            mask = mask_ref[spots, :].astype(f32).astype(bf16)
            seen = jnp.dot(mask, before, preferred_element_type=f32)
            bit = jnp.dot(mask, here, preferred_element_type=f32)
            limit = lax.dot_general(
                limits[:, spots], lead, (((0,), (0,)), ((), ())), preferred_element_type=f32
            )
            kept[spots, :] = jnp.where(seen <= limit, bit, 0.0).astype(bf16)

    arrive(s2)
    z_sum[...] = total(half[pl.ds(aligned(z * quarter, 8), quarter), :], z_rx)
    s3 = spread("y", z_sum, lambda slot: y_rx.at[slot], 4)
    keep(0, chunks)
    arrive(s3)
    y_sum[...] = total(z_sum[...], y_rx)
    s4 = spread("x", y_sum, lambda slot: x_rx.at[slot], 5)
    arrive(wa)
    first_sum[0] = total(weight_half[pl.ds(aligned(y * piece, 16), piece), :], first_rx.at[0])
    wa = scatter("z", first_sum.at[0], 0, small, second_rx.at[0], 11)
    arrive(wb)
    first_sum[1] = total(weight_half[pl.ds(aligned(span + z * piece, 16), piece), :], first_rx.at[1])
    wb = scatter("y", first_sum.at[1], 0, small, second_rx.at[1], 12)
    arrive(s4)
    mine = pl.ds(aligned(core * half_rows + z * quarter, 8), quarter)
    square_ref[mine, :] = total(y_sum[...], x_rx)
    s5 = spread("z", square_ref.at[mine], lambda slot: square_ref.at[mine], 8)
    arrive(p1)
    own_panel = pl.ds(aligned(x * panel_piece, 8), panel_piece)
    panel_ref[own_panel, :] = total(own_rows[own_panel, :], panel_rx)
    p2 = spread("x", panel_ref.at[own_panel], lambda slot: panel_ref.at[own_panel], 9)
    arrive(wa)
    base_a = core * share + y * piece
    base_b = core * share + span + z * piece
    slice_a = pl.ds(aligned(base_a + z * small, 16), small)
    slice_b = pl.ds(aligned(base_b + y * small, 16), small)
    chosen_ref[slice_a, :] = total(first_sum[0, pl.ds(aligned(z * small, 16), small), :], second_rx.at[0])
    wa = spread("z", chosen_ref.at[slice_a], lambda slot: chosen_ref.at[slice_a], 13)
    arrive(wb)
    chosen_ref[slice_b, :] = total(first_sum[1, pl.ds(aligned(y * small, 16), small), :], second_rx.at[1])
    wb = spread("y", chosen_ref.at[slice_b], lambda slot: chosen_ref.at[slice_b], 14)
    arrive(s5)
    own_half = pl.ds(aligned(core * half_rows, 8), half_rows)
    s6 = send(square_ref.at[own_half], square_ref.at[own_half], 10, 0, partner)
    keep(chunks, 2 * chunks)
    arrive(wa)
    piece_a = pl.ds(aligned(base_a, 16), piece)
    wa = spread("y", chosen_ref.at[piece_a], lambda slot: chosen_ref.at[piece_a], 15)
    arrive(wb)
    piece_b = pl.ds(aligned(base_b, 16), piece)
    wb = spread("z", chosen_ref.at[piece_b], lambda slot: chosen_ref.at[piece_b], 16)
    s6.wait_recv()
    own_share = pl.ds(aligned(core * share, 16), share)
    w6 = remote(chosen_ref.at[own_share], chosen_ref.at[own_share], 17, 0, partner)

    def between(t):
        @pl.when(t == 1)
        def _():
            arrive(wa)
            arrive(wb)
            w6.start()

    state[...] = square_ref[...]
    invert(state, right, between)
    arrive(p2)
    coeffs = jnp.dot(state[:, :count], panel_ref[...], precision=HIGHEST, preferred_element_type=f32)
    high[...] = coeffs.astype(bf16)
    low[...] = (coeffs - high[...].astype(f32)).astype(bf16)
    w6.wait_recv()

    def pruned_copy(i):
        spots = pl.ds(aligned(i * chunk, chunk), chunk)
        return pltpu.make_async_copy(pruned_ref.at[spots], pruned_any.at[spots], pruned_sem.at[i])

    def differ(index):
        spots = pl.ds(aligned(index * chunk, chunk), chunk)
        chosen = chosen_ref[spots, :][:, :count]
        change = jnp.dot(chosen, high[...], preferred_element_type=f32)
        change += jnp.dot(chosen, low[...], preferred_element_type=f32)
        wide = weight_ref[spots, :].astype(f32)
        masked = (wide - change) * kept[spots, :].astype(f32)
        pruned_ref[spots, :] = masked.astype(bf16)
        return (wide - masked).astype(bf16)

    diff_copies = {}

    def prepare(k):
        spots = slice(k * chunk, (k + 1) * chunk)
        sent_diff[spots, :] = differ((1 - core) * chunks + k)
        diff_copies[k] = send(sent_diff.at[spots], diff_rx.at[spots], 19, k, partner)
        own_diff[spots, :] = differ(core * chunks + k)

    token_blocks = part.shape[1]

    def multiply(k):
        spots = slice(k * chunk, (k + 1) * chunk)
        tokens = features_ref.shape[0] // token_blocks

        @pl.loop(0, token_blocks)
        def _(t):
            words = pl.ds(aligned(t * tokens, tokens), tokens)
            product = lax.dot_general(
                features_ref[words, :], own_diff[spots, :], (((1,), (1,)), ((), ())), preferred_element_type=f32
            )
            product += lax.dot_general(
                features_rx[words, :], diff_rx[spots, :], (((1,), (1,)), ((), ())), preferred_element_type=f32
            )
            part[k, t] = product.astype(bf16).reshape(part.shape[2:])

    def ring(axis, sent, value, extent, through_rx, through, rx, stage):
        index, device = axes[axis]
        right_one, left_one, across = lax.rem(index + 1, 4), lax.rem(index + 3, 4), lax.rem(index + 2, 4)
        lo, hi = pl.ds(0, extent // 2), pl.ds(extent // 2, extent // 2)
        a = send(sent(across).at[lo], through_rx.at[0], stage, 0, device(right_one))
        b = send(sent(across).at[hi], through_rx.at[1], stage, 1, device(left_one))
        c = send(sent(right_one).at[hi], rx.at[0, hi], stage, 2, device(right_one))
        d = send(sent(left_one).at[lo], rx.at[1, lo], stage, 3, device(left_one))
        later = []

        def pass_on():
            a.wait_recv()
            through[0] = (value(right_one, lo) + through_rx[0].astype(f32)).astype(bf16)
            later.append(send(through.at[0], rx.at[0, lo], stage, 4, device(right_one)))
            b.wait_recv()
            through[1] = (value(left_one, hi) + through_rx[1].astype(f32)).astype(bf16)
            later.append(send(through.at[1], rx.at[1, hi], stage, 5, device(left_one)))

        def finish():
            for copy in (c, d, *later):
                copy.wait_recv()
            return value(index, pl.ds(0, extent)) + rx[0].astype(f32) + rx[1].astype(f32)

        return pass_on, finish

    order = [k for pair in zip(range(chunks // 2), range(chunks // 2, chunks)) for k in pair]
    rings = {}

    def reduce_first(k):
        if k == order[0]:
            features_copy.wait_recv()
        diff_copies[k].wait_recv()
        multiply(k)
        if k < chunks // 2:
            axis = "y"
            sent = functools.partial(lambda k, j: part.at[k, j], k)
        else:
            axis = "z"
            sent = functools.partial(lambda k, j: part.at[k, :, j], k)
        value = functools.partial(lambda sent, j, which: sent(j).at[which][...].astype(f32), sent)
        rings[k] = ring(axis, sent, value, 4, forward_rx.at[k], forward.at[k], ring_rx.at[k], 20 + k)

    prepare(order[0])
    prepare(order[1])
    for n, k in enumerate(order):
        reduce_first(k)
        if n + 2 < chunks:
            prepare(order[n + 2])
    for k in range(2 * chunks):
        pruned_copy(k).start()
    for k in order:
        rings[k][0]()
    again = {}
    for k in order:
        value_sum = rings[k][1]()
        sums_wide[k] = value_sum
        sums[k] = value_sum.astype(bf16)
        axis = "z" if k < chunks // 2 else "y"
        sent = functools.partial(lambda k, j: sums.at[k, j], k)
        value = functools.partial(lambda k, j, which: sums_wide[k, j, which, :], k)
        again[k] = ring(
            axis, sent, value, 64, small_forward_rx.at[k], small_forward.at[k], small_rx.at[k], 20 + chunks + k
        )
    for k in order:
        again[k][0]()
    tokens = error_ref.shape[0]
    last = []
    for k in order:
        final[k] = again[k][1]()
        lanes = pl.ds(aligned(core * share + k * chunk, chunk), chunk)
        last.append(
            send(
                final.at[k, pl.ds(aligned((1 - core) * tokens, tokens), tokens)],
                error_ref.at[:, lanes], 20 + 2 * chunks, k, partner,
            )
        )
        error_ref[:, lanes] = final[k, pl.ds(aligned(core * tokens, tokens), tokens), :]
    for k in range(2 * chunks):
        pruned_copy(k).wait()
    arrive(last)
    w6.wait_send()
    for copy in started:
        copy.wait_send()


def prune(own_rows, line, limit, weight, mask, features, height):
    count, columns = own_rows.shape
    rows = weight.shape[0]
    tokens = features.shape[0]
    f32, bf16 = jnp.float32, jnp.bfloat16
    half, quarter = count // 2, count // 8
    share, chunks = rows // 2, 4
    piece = share // 8
    small = piece // 4
    chunk = share // chunks
    vmem = pl.BlockSpec(memory_space=pltpu.VMEM)
    hbm = pl.BlockSpec(memory_space=pl.ANY)
    stages = 21 + 2 * chunks
    return pl.pallas_call(
        functools.partial(prune_kernel, height=height),
        out_shape=(
            jax.ShapeDtypeStruct((rows, columns), bf16),
            jax.ShapeDtypeStruct((tokens // 32, rows), f32),
        ),
        in_specs=[vmem, vmem, vmem, hbm, hbm, hbm],
        out_specs=(hbm, vmem),
        scratch_shapes=[
            pltpu.VMEM((rows, columns), bf16),
            pltpu.VMEM(mask.shape, jnp.int32),
            pltpu.VMEM(features.shape, bf16),
            pltpu.VMEM((rows, columns), bf16),
            pltpu.VMEM((16, rows), bf16),
            pltpu.VMEM((count, columns), f32),
            pltpu.VMEM((count, LANES), f32),
            pltpu.VMEM((half, LANES), f32),
            pltpu.VMEM((half, LANES), f32),
            pltpu.VMEM((3, quarter, LANES), f32),
            pltpu.VMEM((quarter, LANES), f32),
            pltpu.VMEM((3, quarter, LANES), f32),
            pltpu.VMEM((quarter, LANES), f32),
            pltpu.VMEM((3, quarter, LANES), f32),
            pltpu.VMEM((count, LANES), f32),
            pltpu.VMEM((count, LANES), f32),
            pltpu.VMEM((BLK, LANES), f32),
            pltpu.VMEM((3, count // 4, columns), f32),
            pltpu.VMEM((count, columns), f32),
            pltpu.VMEM((rows, LANES), bf16),
            pltpu.VMEM((share, LANES), bf16),
            pltpu.VMEM((share, LANES), bf16),
            pltpu.VMEM((2, 3, piece, LANES), bf16),
            pltpu.VMEM((2, piece, LANES), bf16),
            pltpu.VMEM((2, 3, small, LANES), bf16),
            pltpu.VMEM((rows, LANES), bf16),
            pltpu.VMEM((count, columns), bf16),
            pltpu.VMEM((count, columns), bf16),
            pltpu.VMEM(features.shape, bf16),
            pltpu.VMEM((share, columns), bf16),
            pltpu.VMEM((share, columns), bf16),
            pltpu.VMEM((share, columns), bf16),
            pltpu.VMEM((rows, columns), bf16),
            pltpu.VMEM((chunks, 4, 4, 64, chunk), bf16),
            pltpu.VMEM((chunks, 2, 2, 64, chunk), bf16),
            pltpu.VMEM((chunks, 2, 2, 64, chunk), bf16),
            pltpu.VMEM((chunks, 2, 4, 64, chunk), bf16),
            pltpu.VMEM((chunks, 4, 64, chunk), bf16),
            pltpu.VMEM((chunks, 4, 64, chunk), f32),
            pltpu.VMEM((chunks, 2, 32, chunk), bf16),
            pltpu.VMEM((chunks, 2, 32, chunk), bf16),
            pltpu.VMEM((chunks, 2, 64, chunk), bf16),
            pltpu.VMEM((chunks, 64, chunk), f32),
            pltpu.SemaphoreType.DMA((stages, 6)),
            pltpu.SemaphoreType.DMA((stages, 6)),
            pltpu.SemaphoreType.DMA((3,)),
            pltpu.SemaphoreType.DMA((2 * chunks,)),
        ],
        compiler_params=pltpu.CompilerParams(
            collective_id=0, has_side_effects=True, vmem_limit_bytes=56 << 20
        ),
        name="prune",
    )(own_rows, line, limit, weight, mask, features)


def local(weight, hess_inv, selected, block_mask, row_limits, calibration):
    rows_local = hess_inv.shape[0]
    row_offset = (lax.axis_index("rows") * rows_local).astype(jnp.int32).reshape(1)
    own_rows, line = gather(row_offset, selected, hess_inv)
    pruned, error = prune(
        own_rows, line, row_limits.reshape(1, -1), weight, block_mask, calibration, rows_local
    )
    return (pruned, error.T)


def solution(mesh):
    placed = (
        P("rows", "cols"),
        P("rows", "cols"),
        P(),
        P("rows", None),
        P("rows"),
        P(None, "cols"),
    )
    return jax.shard_map(
        local,
        mesh=mesh,
        in_specs=placed,
        out_specs=(P("rows", "cols"), P("rows", "cols")),
        check_vma=False,
    )
```

```python
import functools

import jax
import jax.numpy as jnp
from jax import lax
from jax.experimental import pallas as pl
from jax.experimental.pallas import tpu as pltpu
from jax.sharding import PartitionSpec as P

BLK = 128
LANES = 256
MESH = pl.DeviceIdType.MESH
HIGHEST = lax.Precision.HIGHEST


def aligned(value, factor):
    return pl.multiple_of(value, factor)


def place():
    row = lax.axis_index("rows")
    col = lax.axis_index("cols")
    core = lax.rem(col, 2)
    z = lax.rem(col // 2, 4)
    y = col // 8
    partner = (row, col + 1 - 2 * core)
    axes = {
        "x": (row, lambda j: (j, col)),
        "y": (y, lambda j: (row, (j * 4 + z) * 2 + core)),
        "z": (z, lambda j: (row, (y * 4 + j) * 2 + core)),
    }
    return core, partner, axes


def enter(partner, axes):
    barrier = pltpu.get_barrier_semaphore()
    pl.semaphore_signal(barrier, inc=1, device_id=partner, device_id_type=MESH)
    for index, device in axes.values():
        for step in (1, 2, 3):
            pl.semaphore_signal(
                barrier, inc=1, device_id=device(lax.rem(index + step, 4)), device_id_type=MESH
            )
    pl.semaphore_wait(barrier, 1 + 3 * len(axes))


def gather_kernel(offset_ref, selected_ref, values_ref, inverse_ref, own_ref, line_ref, sem):
    steps, width = selected_ref.shape
    height = inverse_ref.shape[0]
    def row_copy(spot, k):
        return pltpu.make_async_copy(inverse_ref.at[pl.ds(spot, 1)], own_ref.at[pl.ds(k, 1)], sem)

    owned = 0
    for step in range(steps):

        def start(k, owned):
            spot = selected_ref[step, k] - offset_ref[0]
            inside = (spot >= 0) & (spot < height)

            @pl.when(inside)
            def _():
                row_copy(spot, step * width + k).start()

            return owned + jnp.where(inside, 1, 0)

        owned = lax.fori_loop(0, width, start, owned, unroll=8)
    line_ref[...] = jnp.full(line_ref.shape, -1, jnp.int32)
    for step in range(steps):
        line_ref[0:1, step * width : (step + 1) * width] = values_ref[step : step + 1, :]

    def finish(k, carry):
        row_copy(0, 0).wait()
        return carry

    lax.fori_loop(0, owned, finish, 0)


def gather(offset, selected, inverse):
    count = selected.size
    smem = pl.BlockSpec(memory_space=pltpu.SMEM)
    vmem = pl.BlockSpec(memory_space=pltpu.VMEM)
    return pl.pallas_call(
        gather_kernel,
        out_shape=(
            jax.ShapeDtypeStruct((count, inverse.shape[1]), jnp.float32),
            jax.ShapeDtypeStruct((8, LANES), jnp.int32),
        ),
        in_specs=[smem, smem, vmem, pl.BlockSpec(memory_space=pl.ANY)],
        out_specs=(vmem, vmem),
        scratch_shapes=[pltpu.SemaphoreType.DMA],
        name="gather",
    )(offset, selected, selected, inverse)


def invert(state, right, between):
    count, width = state.shape
    size, side = 8, 64
    blocks = side // size
    lane = lax.broadcasted_iota(jnp.int32, (size, BLK), 1)
    line = lax.broadcasted_iota(jnp.int32, (size, BLK), 0)

    def column(tile, k):
        return jnp.broadcast_to(tile[:, k : k + 1], tile.shape)

    def row(tile, k):
        return jnp.broadcast_to(tile[k : k + 1, :], tile.shape)

    def fold(parts):
        while len(parts) > 1:
            parts = [parts[i] + parts[i + 1] for i in range(0, len(parts), 2)]
        return parts[0]

    def step(t, carry):
        half = t // 2
        shift = (t - half * 2) * side
        lanes = pl.ds(aligned(half * BLK, BLK), BLK)
        lines = pl.ds(aligned(t * side, side), side)
        moved = jnp.where(shift > 0, pltpu.roll(state[lines, lanes], side, 1), state[lines, lanes])
        groups = [moved[i * size : (i + 1) * size] for i in range(blocks)]
        for b in range(blocks):
            at = b * size
            pivot = [column(groups[b], at + j) for j in range(size)]
            for k in range(size):
                scale = 1.0 / row(pivot[k], k)
                lead = pivot[k]
                for j in range(size):
                    if j != k:
                        scaled = row(pivot[j], k) * scale
                        pivot[j] = jnp.where(line == k, scaled, pivot[j] - lead * scaled)
                pivot[k] = jnp.where(line == k, scale, -lead * scale)
            inside = (lane >= at) & (lane < at + size)
            tile = jnp.where(inside, jnp.where(lane - at == line, 1.0, 0.0), groups[b])
            fresh = fold([pivot[j] * row(tile, j) for j in range(size)])
            rows = [row(fresh, j) for j in range(size)]
            order = [(b + 1 + i) % blocks for i in range(blocks - 1)]
            for i in order:
                change = fold([column(groups[i], at + j) * rows[j] for j in range(size)])
                groups[i] = jnp.where(inside, 0.0, groups[i]) - change
            groups[b] = fresh
        block = jnp.concatenate(groups, axis=0)[:, :side]
        own = pl.ds(aligned(shift, side), side)
        wide = lax.broadcasted_iota(jnp.int32, (side, width), 1) - t * side
        unit = jnp.where(wide == lax.broadcasted_iota(jnp.int32, (side, width), 0), 1.0, 0.0)
        solved = jnp.dot(
            block, jnp.where((wide >= 0) & (wide < side), unit, state[lines, :]),
            precision=HIGHEST, preferred_element_type=jnp.float32,
        )
        right[...] = jnp.zeros(right.shape, jnp.float32)
        right[own, :] = solved
        tall = lax.broadcasted_iota(jnp.int32, (count, BLK), 1)
        strip = jnp.where((tall >= shift) & (tall < shift + side), state[:, lanes], 0.0)
        spans = lax.broadcasted_iota(jnp.int32, (count, width), 1) - t * side
        cleared = jnp.where((spans >= 0) & (spans < side), 0.0, state[...])
        state[...] = cleared - jnp.dot(strip, right[...], precision=HIGHEST, preferred_element_type=jnp.float32)
        state[lines, :] = solved
        between(t)
        return carry

    lax.fori_loop(0, count // side, step, 0)


def prune_kernel(
    own_ref, line_ref, limit_ref, weight_any, mask_any, features_any, pruned_any, error_ref,
    weight_ref, mask_ref, features_ref, kept, limits,
    own_rows, square_part, half_rx, half, z_rx, z_sum, y_rx, y_sum, x_rx, square_ref, state, right,
    panel_rx, panel_ref, weight_part, weight_rx, weight_half, first_rx, first_sum, second_rx, chosen_ref,
    high, low, features_rx, own_diff, sent_diff, diff_rx, pruned_ref, part, forward_rx, forward, ring_rx,
    sums, sums_wide, small_forward_rx, small_forward, small_rx, final,
    send_sem, recv_sem, local_sem, pruned_sem,
    *, height,
):
    core, partner, axes = place()
    rows, columns = weight_ref.shape
    col_offset = lax.axis_index("cols") * columns
    count = own_ref.shape[0]
    half_rows = count // 2
    quarter = half_rows // 4
    share = rows // 2
    chunks = part.shape[0]
    chunk = share // chunks
    blocks = columns // BLK
    f32, bf16 = jnp.float32, jnp.bfloat16
    loads = [
        pltpu.make_async_copy(src, dst, local_sem.at[i])
        for i, (src, dst) in enumerate(
            ((weight_any, weight_ref), (features_any, features_ref), (mask_any, mask_ref))
        )
    ]
    for load in loads:
        load.start()

    sent = {}

    def remote(src, dst, arrival, group, device):
        return pltpu.make_async_remote_copy(
            src_ref=src, dst_ref=dst, send_sem=send_sem.at[group], recv_sem=recv_sem.at[arrival],
            device_id=device, device_id_type=MESH,
        )

    def send(src, dst, arrival, group, device):
        remote(src, dst, arrival, group, device).start()
        size = jnp.dtype(src.dtype).itemsize
        for extent in src.shape:
            size *= extent
        sent[group] = sent.get(group, 0) + size

    def arrive(view, arrival):
        remote(view, view, arrival, 0, partner).wait_recv()

    def scatter(axis, src, base, piece, rx, arrival, group):
        index, device = axes[axis]
        for step in (1, 2, 3):
            peer = lax.rem(index + step, 4)
            start = aligned(base + peer * piece, 8)
            send(src.at[pl.ds(start, piece)], rx.at[step - 1], arrival, group, device(peer))

    def spread(axis, src, dst_of, arrival, group):
        index, device = axes[axis]
        for step in (1, 2, 3):
            send(src, dst_of(step - 1), arrival, group, device(lax.rem(index + step, 4)))

    def total(own, rx):
        return own + rx[0] + rx[1] + rx[2]

    row_offset = lax.axis_index("rows") * height
    picked = line_ref[0:1, :count]
    owned = jnp.where((picked >= row_offset) & (picked < row_offset + height), 1.0, 0.0)
    first = lax.broadcasted_iota(jnp.int32, (16, count), 0) == 0
    owned = lax.dot_general(
        jnp.where(first, owned, 0.0).astype(bf16), jnp.ones((16, columns), bf16),
        (((0,), (0,)), ((), ())), preferred_element_type=f32,
    )
    own_rows[...] = jnp.where(owned > 0.5, own_ref[...], 0.0)
    lines = lax.broadcasted_iota(jnp.int32, (columns, LANES), 0) + col_offset
    onehot = jnp.where(lines == line_ref[0:1, :], 1.0, 0.0)
    square_part[...] = jnp.dot(own_rows[...], onehot, precision=HIGHEST, preferred_element_type=f32)

    enter(partner, axes)
    x, y, z = axes["x"][0], axes["y"][0], axes["z"][0]
    send(square_part.at[pl.ds(aligned((1 - core) * half_rows, 8), half_rows)], half_rx, 0, 0, partner)
    panel_piece = count // 4
    scatter("x", own_rows, 0, panel_piece, panel_rx, 1, 0)
    loads[0].wait()
    weight_part[...] = jnp.dot(weight_ref[...], onehot.astype(bf16), preferred_element_type=f32).astype(bf16)
    send(weight_part.at[pl.ds(aligned((1 - core) * share, 16), share)], weight_rx, 2, 1, partner)
    arrive(half_rx, 0)
    half[...] = square_part[pl.ds(aligned(core * half_rows, 8), half_rows), :] + half_rx[...]
    scatter("z", half, 0, quarter, z_rx, 3, 0)
    loads[1].wait()
    send(features_ref, features_rx, 18, 2, partner)
    arrive(weight_rx, 2)
    weight_half[...] = weight_part[pl.ds(aligned(core * share, 16), share), :] + weight_rx[...]
    span = share // 2
    piece = span // 4
    small = piece // 4
    scatter("y", weight_half, 0, piece, first_rx.at[0], 6, 1)
    scatter("z", weight_half, span, piece, first_rx.at[1], 7, 1)

    loads[2].wait()
    limits[...] = jnp.broadcast_to(limit_ref[0:1, :].astype(f32), limits.shape).astype(bf16)
    place_line = lax.broadcasted_iota(jnp.int32, (BLK, columns), 0)
    block = lax.axis_index("cols") * blocks + lax.broadcasted_iota(jnp.int32, (BLK, columns), 1) // BLK
    before = jnp.where(place_line <= block, 1.0, 0.0).astype(bf16)
    here = jnp.where(place_line == block, 1.0, 0.0).astype(bf16)
    lead = jnp.where(lax.broadcasted_iota(jnp.int32, (16, columns), 0) == 0, 1.0, 0.0).astype(bf16)

    def keep(low_chunk, high_chunk):
        @pl.loop(low_chunk, high_chunk)
        def _(i):
            spots = pl.ds(aligned(i * chunk, chunk), chunk)
            mask = mask_ref[spots, :].astype(f32).astype(bf16)
            seen = jnp.dot(mask, before, preferred_element_type=f32)
            bit = jnp.dot(mask, here, preferred_element_type=f32)
            limit = lax.dot_general(
                limits[:, spots], lead, (((0,), (0,)), ((), ())), preferred_element_type=f32
            )
            kept[spots, :] = jnp.where(seen <= limit, bit, 0.0).astype(bf16)

    arrive(z_rx, 3)
    z_sum[...] = total(half[pl.ds(aligned(z * quarter, 8), quarter), :], z_rx)
    spread("y", z_sum, lambda slot: y_rx.at[slot], 4, 0)
    keep(0, chunks)
    arrive(y_rx, 4)
    y_sum[...] = total(z_sum[...], y_rx)
    spread("x", y_sum, lambda slot: x_rx.at[slot], 5, 0)
    arrive(first_rx.at[0], 6)
    first_sum[0] = total(weight_half[pl.ds(aligned(y * piece, 16), piece), :], first_rx.at[0])
    scatter("z", first_sum.at[0], 0, small, second_rx.at[0], 11, 1)
    arrive(first_rx.at[1], 7)
    first_sum[1] = total(weight_half[pl.ds(aligned(span + z * piece, 16), piece), :], first_rx.at[1])
    scatter("y", first_sum.at[1], 0, small, second_rx.at[1], 12, 1)
    arrive(x_rx, 5)
    mine = pl.ds(aligned(core * half_rows + z * quarter, 8), quarter)
    square_ref[mine, :] = total(y_sum[...], x_rx)
    spread("z", square_ref.at[mine], lambda slot: square_ref.at[mine], 8, 0)
    arrive(panel_rx, 1)
    own_panel = pl.ds(aligned(x * panel_piece, 8), panel_piece)
    panel_ref[own_panel, :] = total(own_rows[own_panel, :], panel_rx)
    spread("x", panel_ref.at[own_panel], lambda slot: panel_ref.at[own_panel], 9, 0)
    arrive(second_rx.at[0], 11)
    base_a = core * share + y * piece
    base_b = core * share + span + z * piece
    slice_a = pl.ds(aligned(base_a + z * small, 16), small)
    slice_b = pl.ds(aligned(base_b + y * small, 16), small)
    chosen_ref[slice_a, :] = total(first_sum[0, pl.ds(aligned(z * small, 16), small), :], second_rx.at[0])
    spread("z", chosen_ref.at[slice_a], lambda slot: chosen_ref.at[slice_a], 13, 1)
    arrive(second_rx.at[1], 12)
    chosen_ref[slice_b, :] = total(first_sum[1, pl.ds(aligned(y * small, 16), small), :], second_rx.at[1])
    spread("y", chosen_ref.at[slice_b], lambda slot: chosen_ref.at[slice_b], 14, 1)
    arrive(square_ref.at[pl.ds(0, 3 * quarter)], 8)
    own_half = pl.ds(aligned(core * half_rows, 8), half_rows)
    send(square_ref.at[own_half], square_ref.at[own_half], 10, 0, partner)
    keep(chunks, 2 * chunks)
    arrive(chosen_ref.at[pl.ds(0, 3 * small)], 13)
    piece_a = pl.ds(aligned(base_a, 16), piece)
    spread("y", chosen_ref.at[piece_a], lambda slot: chosen_ref.at[piece_a], 15, 1)
    arrive(chosen_ref.at[pl.ds(0, 3 * small)], 14)
    piece_b = pl.ds(aligned(base_b, 16), piece)
    spread("z", chosen_ref.at[piece_b], lambda slot: chosen_ref.at[piece_b], 16, 1)
    arrive(square_ref.at[pl.ds(0, half_rows)], 10)
    own_share = pl.ds(aligned(core * share, 16), share)

    def between(t):
        @pl.when(t == 1)
        def _():
            arrive(chosen_ref.at[pl.ds(0, 3 * piece)], 15)
            arrive(chosen_ref.at[pl.ds(0, 3 * piece)], 16)
            send(chosen_ref.at[own_share], chosen_ref.at[own_share], 17, 1, partner)

    state[...] = square_ref[...]
    invert(state, right, between)
    arrive(panel_ref.at[pl.ds(0, 3 * panel_piece)], 9)
    coeffs = jnp.dot(state[:, :count], panel_ref[...], precision=HIGHEST, preferred_element_type=f32)
    high[...] = coeffs.astype(bf16)
    low[...] = (coeffs - high[...].astype(f32)).astype(bf16)
    arrive(chosen_ref.at[pl.ds(0, share)], 17)

    def pruned_copy(i):
        spots = pl.ds(aligned(i * chunk, chunk), chunk)
        return pltpu.make_async_copy(pruned_ref.at[spots], pruned_any.at[spots], pruned_sem)

    def differ(index):
        spots = pl.ds(aligned(index * chunk, chunk), chunk)
        chosen = chosen_ref[spots, :][:, :count]
        change = jnp.dot(chosen, high[...], preferred_element_type=f32)
        change += jnp.dot(chosen, low[...], preferred_element_type=f32)
        wide = weight_ref[spots, :].astype(f32)
        masked = (wide - change) * kept[spots, :].astype(f32)
        pruned_ref[spots, :] = masked.astype(bf16)
        return (wide - masked).astype(bf16)

    def prepare(k):
        spots = slice(k * chunk, (k + 1) * chunk)
        sent_diff[spots, :] = differ((1 - core) * chunks + k)
        send(sent_diff.at[spots], diff_rx.at[spots], 20 + k, 2, partner)
        own_diff[spots, :] = differ(core * chunks + k)

    token_blocks = part.shape[1]

    def multiply(k):
        spots = slice(k * chunk, (k + 1) * chunk)
        tokens = features_ref.shape[0] // token_blocks

        @pl.loop(0, token_blocks)
        def _(t):
            words = pl.ds(aligned(t * tokens, tokens), tokens)
            product = lax.dot_general(
                features_ref[words, :], own_diff[spots, :], (((1,), (1,)), ((), ())), preferred_element_type=f32
            )
            product += lax.dot_general(
                features_rx[words, :], diff_rx[spots, :], (((1,), (1,)), ((), ())), preferred_element_type=f32
            )
            part[k, t] = product.astype(bf16).reshape(part.shape[2:])

    def ring(axis, parcel, value, extent, through_rx, through, rx, first):
        index, device = axes[axis]
        right_one, left_one, across = lax.rem(index + 1, 4), lax.rem(index + 3, 4), lax.rem(index + 2, 4)
        lo, hi = pl.ds(0, extent // 2), pl.ds(extent // 2, extent // 2)
        send(parcel(across).at[lo], through_rx.at[0], first, 3, device(right_one))
        send(parcel(across).at[hi], through_rx.at[1], first + 1, 3, device(left_one))
        send(parcel(right_one).at[hi], rx.at[0, hi], first + 2, 3, device(right_one))
        send(parcel(left_one).at[lo], rx.at[1, lo], first + 2, 3, device(left_one))

        def pass_on():
            arrive(through_rx.at[0], first)
            through[0] = (value(right_one, lo) + through_rx[0].astype(f32)).astype(bf16)
            send(through.at[0], rx.at[0, lo], first + 2, 3, device(right_one))
            arrive(through_rx.at[1], first + 1)
            through[1] = (value(left_one, hi) + through_rx[1].astype(f32)).astype(bf16)
            send(through.at[1], rx.at[1, hi], first + 2, 3, device(left_one))

        def finish():
            arrive(rx, first + 2)
            return value(index, pl.ds(0, extent)) + rx[0].astype(f32) + rx[1].astype(f32)

        return pass_on, finish

    order = [k for pair in zip(range(chunks // 2), range(chunks // 2, chunks)) for k in pair]
    rings = {}

    def reduce_first(k):
        if k == order[0]:
            arrive(features_rx, 18)
        arrive(diff_rx.at[k * chunk : (k + 1) * chunk], 20 + k)
        multiply(k)
        if k < chunks // 2:
            axis = "y"
            parcel = functools.partial(lambda k, j: part.at[k, j], k)
        else:
            axis = "z"
            parcel = functools.partial(lambda k, j: part.at[k, :, j], k)
        value = functools.partial(lambda parcel, j, which: parcel(j).at[which][...].astype(f32), parcel)
        rings[k] = ring(axis, parcel, value, 4, forward_rx.at[k], forward.at[k], ring_rx.at[k], 24 + 3 * k)

    prepare(order[0])
    prepare(order[1])
    for n, k in enumerate(order):
        reduce_first(k)
        if n + 2 < chunks:
            prepare(order[n + 2])
    for k in range(2 * chunks):
        pruned_copy(k).start()
    for k in order:
        rings[k][0]()
    again = {}
    for k in order:
        value_sum = rings[k][1]()
        sums_wide[k] = value_sum
        sums[k] = value_sum.astype(bf16)
        axis = "z" if k < chunks // 2 else "y"
        parcel = functools.partial(lambda k, j: sums.at[k, j], k)
        value = functools.partial(lambda k, j, which: sums_wide[k, j, which, :], k)
        again[k] = ring(
            axis, parcel, value, 64, small_forward_rx.at[k], small_forward.at[k], small_rx.at[k],
            24 + 3 * (chunks + k),
        )
    for k in order:
        again[k][0]()
    tokens = error_ref.shape[0]
    for k in order:
        final[k] = again[k][1]()
        lanes = pl.ds(aligned(core * share + k * chunk, chunk), chunk)
        send(
            final.at[k, pl.ds(aligned((1 - core) * tokens, tokens), tokens)], error_ref.at[:, lanes], 19, 0, partner
        )
        error_ref[:, lanes] = final[k, pl.ds(aligned(core * tokens, tokens), tokens), :]
    pltpu.make_async_copy(pruned_ref, pruned_any, pruned_sem).wait()
    arrive(error_ref.at[:, pl.ds(0, share)], 19)
    unit_bytes = columns * jnp.dtype(weight_ref.dtype).itemsize
    for group, size in sent.items():
        view = weight_ref.at[pl.ds(0, size // unit_bytes)]
        remote(view, view, 0, group, partner).wait_send()


def prune(own_rows, line, limit, weight, mask, features, height):
    count, columns = own_rows.shape
    rows = weight.shape[0]
    tokens = features.shape[0]
    f32, bf16 = jnp.float32, jnp.bfloat16
    half, quarter = count // 2, count // 8
    share, chunks = rows // 2, 4
    piece = share // 8
    small = piece // 4
    chunk = share // chunks
    vmem = pl.BlockSpec(memory_space=pltpu.VMEM)
    hbm = pl.BlockSpec(memory_space=pl.ANY)
    arrivals = 24 + 6 * chunks
    return pl.pallas_call(
        functools.partial(prune_kernel, height=height),
        out_shape=(
            jax.ShapeDtypeStruct((rows, columns), bf16),
            jax.ShapeDtypeStruct((tokens // 32, rows), f32),
        ),
        in_specs=[vmem, vmem, vmem, hbm, hbm, hbm],
        out_specs=(hbm, vmem),
        scratch_shapes=[
            pltpu.VMEM((rows, columns), bf16),
            pltpu.VMEM(mask.shape, jnp.int32),
            pltpu.VMEM(features.shape, bf16),
            pltpu.VMEM((rows, columns), bf16),
            pltpu.VMEM((16, rows), bf16),
            pltpu.VMEM((count, columns), f32),
            pltpu.VMEM((count, LANES), f32),
            pltpu.VMEM((half, LANES), f32),
            pltpu.VMEM((half, LANES), f32),
            pltpu.VMEM((3, quarter, LANES), f32),
            pltpu.VMEM((quarter, LANES), f32),
            pltpu.VMEM((3, quarter, LANES), f32),
            pltpu.VMEM((quarter, LANES), f32),
            pltpu.VMEM((3, quarter, LANES), f32),
            pltpu.VMEM((count, LANES), f32),
            pltpu.VMEM((count, LANES), f32),
            pltpu.VMEM((BLK, LANES), f32),
            pltpu.VMEM((3, count // 4, columns), f32),
            pltpu.VMEM((count, columns), f32),
            pltpu.VMEM((rows, LANES), bf16),
            pltpu.VMEM((share, LANES), bf16),
            pltpu.VMEM((share, LANES), bf16),
            pltpu.VMEM((2, 3, piece, LANES), bf16),
            pltpu.VMEM((2, piece, LANES), bf16),
            pltpu.VMEM((2, 3, small, LANES), bf16),
            pltpu.VMEM((rows, LANES), bf16),
            pltpu.VMEM((count, columns), bf16),
            pltpu.VMEM((count, columns), bf16),
            pltpu.VMEM(features.shape, bf16),
            pltpu.VMEM((share, columns), bf16),
            pltpu.VMEM((share, columns), bf16),
            pltpu.VMEM((share, columns), bf16),
            pltpu.VMEM((rows, columns), bf16),
            pltpu.VMEM((chunks, 4, 4, 64, chunk), bf16),
            pltpu.VMEM((chunks, 2, 2, 64, chunk), bf16),
            pltpu.VMEM((chunks, 2, 2, 64, chunk), bf16),
            pltpu.VMEM((chunks, 2, 4, 64, chunk), bf16),
            pltpu.VMEM((chunks, 4, 64, chunk), bf16),
            pltpu.VMEM((chunks, 4, 64, chunk), f32),
            pltpu.VMEM((chunks, 2, 32, chunk), bf16),
            pltpu.VMEM((chunks, 2, 32, chunk), bf16),
            pltpu.VMEM((chunks, 2, 64, chunk), bf16),
            pltpu.VMEM((chunks, 64, chunk), f32),
            pltpu.SemaphoreType.DMA((4,)),
            pltpu.SemaphoreType.DMA((arrivals,)),
            pltpu.SemaphoreType.DMA((3,)),
            pltpu.SemaphoreType.DMA,
        ],
        compiler_params=pltpu.CompilerParams(
            collective_id=0, has_side_effects=True, vmem_limit_bytes=56 << 20
        ),
        name="prune",
    )(own_rows, line, limit, weight, mask, features)


def local(weight, hess_inv, selected, block_mask, row_limits, calibration):
    rows_local = hess_inv.shape[0]
    row_offset = (lax.axis_index("rows") * rows_local).astype(jnp.int32).reshape(1)
    own_rows, line = gather(row_offset, selected, hess_inv)
    pruned, error = prune(
        own_rows, line, row_limits.reshape(1, -1), weight, block_mask, calibration, rows_local
    )
    return (pruned, error.T)


def solution(mesh):
    placed = (
        P("rows", "cols"),
        P("rows", "cols"),
        P(),
        P("rows", None),
        P("rows"),
        P(None, "cols"),
    )
    return jax.shard_map(
        local,
        mesh=mesh,
        in_specs=placed,
        out_specs=(P("rows", "cols"), P("rows", "cols")),
        check_vma=False,
    )
```

```python
import functools

import jax
import jax.numpy as jnp
from jax import lax
from jax.experimental import pallas as pl
from jax.experimental.pallas import tpu as pltpu
from jax.sharding import PartitionSpec as P

BLK = 128
LANES = 256
MESH = pl.DeviceIdType.MESH
HIGHEST = lax.Precision.HIGHEST


def aligned(value, factor):
    return pl.multiple_of(value, factor)


def place():
    row = lax.axis_index("rows")
    col = lax.axis_index("cols")
    core = lax.rem(col, 2)
    z = lax.rem(col // 2, 4)
    y = col // 8
    partner = (row, col + 1 - 2 * core)
    axes = {
        "x": (row, lambda j, k=core: (j, (y * 4 + z) * 2 + k)),
        "y": (y, lambda j, k=core: (row, (j * 4 + z) * 2 + k)),
        "z": (z, lambda j, k=core: (row, (y * 4 + j) * 2 + k)),
    }
    return core, partner, axes


def enter(core, partner, axes):
    barrier = pltpu.get_barrier_semaphore()
    greeted = [partner]
    for name, (index, device) in axes.items():
        for step in (1, 2, 3):
            peer = lax.rem(index + step, 4)
            greeted.append(device(peer))
            if name != "x":
                greeted.append(device(peer, 1 - core))
    for other in greeted:
        pl.semaphore_signal(barrier, inc=1, device_id=other, device_id_type=MESH)
    pl.semaphore_wait(barrier, len(greeted))


def gather_kernel(offset_ref, selected_ref, values_ref, inverse_ref, own_ref, line_ref, sem):
    steps, width = selected_ref.shape
    height = inverse_ref.shape[0]
    def row_copy(spot, k):
        return pltpu.make_async_copy(inverse_ref.at[pl.ds(spot, 1)], own_ref.at[pl.ds(k, 1)], sem)

    owned = 0
    for step in range(steps):

        def start(k, owned):
            spot = selected_ref[step, k] - offset_ref[0]
            inside = (spot >= 0) & (spot < height)

            @pl.when(inside)
            def _():
                row_copy(spot, step * width + k).start()

            return owned + jnp.where(inside, 1, 0)

        owned = lax.fori_loop(0, width, start, owned, unroll=8)
    line_ref[...] = jnp.full(line_ref.shape, -1, jnp.int32)
    for step in range(steps):
        line_ref[0:1, step * width : (step + 1) * width] = values_ref[step : step + 1, :]

    def finish(k, carry):
        row_copy(0, 0).wait()
        return carry

    lax.fori_loop(0, owned, finish, 0)


def gather(offset, selected, inverse):
    count = selected.size
    smem = pl.BlockSpec(memory_space=pltpu.SMEM)
    vmem = pl.BlockSpec(memory_space=pltpu.VMEM)
    return pl.pallas_call(
        gather_kernel,
        out_shape=(
            jax.ShapeDtypeStruct((count, inverse.shape[1]), jnp.float32),
            jax.ShapeDtypeStruct((8, LANES), jnp.int32),
        ),
        in_specs=[smem, smem, vmem, pl.BlockSpec(memory_space=pl.ANY)],
        out_specs=(vmem, vmem),
        scratch_shapes=[pltpu.SemaphoreType.DMA],
        name="gather",
    )(offset, selected, selected, inverse)


def invert(state, right, between):
    count, width = state.shape
    size, side = 8, 64
    blocks = side // size
    lane = lax.broadcasted_iota(jnp.int32, (size, BLK), 1)
    line = lax.broadcasted_iota(jnp.int32, (size, BLK), 0)

    def column(tile, at):
        picked = jnp.where(lane == at, tile, 0.0)
        return jnp.broadcast_to(jnp.sum(picked, axis=1, keepdims=True), tile.shape)

    def row(tile, k):
        return jnp.broadcast_to(tile[k : k + 1, :], tile.shape)

    def fold(parts):
        while len(parts) > 1:
            parts = [parts[i] + parts[i + 1] for i in range(0, len(parts), 2)]
        return parts[0]

    def step(t, carry):
        half = t // 2
        shift = (t - half * 2) * side
        lanes = pl.ds(aligned(half * BLK, BLK), BLK)
        groups = [state[pl.ds(aligned(t * side + i * size, size), size), lanes] for i in range(blocks)]
        for b in range(blocks):
            at = shift + b * size
            pivot = [column(groups[b], at + j) for j in range(size)]
            for k in range(size):
                scale = 1.0 / row(pivot[k], k)
                lead = pivot[k]
                for j in range(size):
                    if j != k:
                        scaled = row(pivot[j], k) * scale
                        pivot[j] = jnp.where(line == k, scaled, pivot[j] - lead * scaled)
                pivot[k] = jnp.where(line == k, scale, -lead * scale)
            inside = (lane >= at) & (lane < at + size)
            tile = jnp.where(inside, jnp.where(lane - at == line, 1.0, 0.0), groups[b])
            fresh = fold([pivot[j] * row(tile, j) for j in range(size)])
            rows = [row(fresh, j) for j in range(size)]
            order = [(b + 1 + i) % blocks for i in range(blocks - 1)]
            for i in order:
                change = fold([column(groups[i], at + j) * rows[j] for j in range(size)])
                groups[i] = jnp.where(inside, 0.0, groups[i]) - change
            groups[b] = fresh
        mine = (lane >= shift) & (lane < shift + side)
        block = jnp.concatenate([jnp.where(mine, group, 0.0) for group in groups], axis=0)
        own = pl.ds(aligned(shift, side), side)
        lines = pl.ds(aligned(t * side, side), side)
        wide = lax.broadcasted_iota(jnp.int32, (side, width), 1) - t * side
        unit = jnp.where(wide == lax.broadcasted_iota(jnp.int32, (side, width), 0), 1.0, 0.0)
        right[...] = jnp.zeros(right.shape, jnp.float32)
        right[own, :] = jnp.where((wide >= 0) & (wide < side), unit, state[lines, :])
        solved = jnp.dot(block, right[...], precision=HIGHEST, preferred_element_type=jnp.float32)
        right[own, :] = solved
        tall = lax.broadcasted_iota(jnp.int32, (count, BLK), 1)
        strip = jnp.where((tall >= shift) & (tall < shift + side), state[:, lanes], 0.0)
        spans = lax.broadcasted_iota(jnp.int32, (count, width), 1) - t * side
        cleared = jnp.where((spans >= 0) & (spans < side), 0.0, state[...])
        state[...] = cleared - jnp.dot(strip, right[...], precision=HIGHEST, preferred_element_type=jnp.float32)
        state[lines, :] = solved
        between(t)
        return carry

    lax.fori_loop(0, count // side, step, 0)


def prune_kernel(
    own_ref, line_ref, limit_ref, weight_any, mask_any, features_any, pruned_any, error_ref,
    weight_ref, mask_ref, features_ref, kept, limits,
    own_rows, square_part, z_rx, z_sum, y_rx, y_sum, x_rx, square_ref, state, right,
    panel_rx, panel_ref, weight_part, weight_rx, weight_half, first_rx, first_sum, second_rx, chosen_ref,
    high, low, features_rx, own_diff, sent_diff, diff_rx, pruned_ref, part, forward_rx, forward, ring_rx,
    sums, sums_wide, last_rx,
    send_sem, recv_sem, local_sem, pruned_sem,
    *, height,
):
    core, partner, axes = place()
    rows, columns = weight_ref.shape
    col_offset = lax.axis_index("cols") * columns
    count = own_ref.shape[0]
    quarter = count // 8
    share = rows // 2
    chunks = part.shape[0]
    chunk = share // chunks
    blocks = columns // BLK
    f32, bf16 = jnp.float32, jnp.bfloat16
    loads = [
        pltpu.make_async_copy(src, dst, local_sem.at[i])
        for i, (src, dst) in enumerate(
            ((weight_any, weight_ref), (features_any, features_ref), (mask_any, mask_ref))
        )
    ]
    for load in loads:
        load.start()

    sent = {}

    def remote(src, dst, arrival, group, device):
        return pltpu.make_async_remote_copy(
            src_ref=src, dst_ref=dst, send_sem=send_sem.at[group], recv_sem=recv_sem.at[arrival],
            device_id=device, device_id_type=MESH,
        )

    def send(src, dst, arrival, group, device):
        remote(src, dst, arrival, group, device).start()
        size = jnp.dtype(src.dtype).itemsize
        for extent in src.shape:
            size *= extent
        sent[group] = sent.get(group, 0) + size

    def arrive(view, arrival):
        remote(view, view, arrival, 0, partner).wait_recv()

    def scatter(axis, src, base, piece, rx, arrival, group):
        index, device = axes[axis]
        for step in (1, 2, 3):
            peer = lax.rem(index + step, 4)
            start = aligned(base + peer * piece, 8)
            send(src.at[pl.ds(start, piece)], rx.at[step - 1], arrival, group, device(peer))

    def spread(axis, src, dst_of, arrival, group):
        index, device = axes[axis]
        for step in (1, 2, 3):
            send(src, dst_of(step - 1), arrival, group, device(lax.rem(index + step, 4)))

    def around(index):
        for step in range(4):
            for turn in range(2):
                if step + turn > 0:
                    yield 2 * step + turn - 1, lax.rem(index + step, 4), lax.rem(core + turn, 2)

    def total(own, rx):
        return own + rx[0] + rx[1] + rx[2]

    row_offset = lax.axis_index("rows") * height
    picked = line_ref[0:1, :count]
    owned = jnp.where((picked >= row_offset) & (picked < row_offset + height), 1.0, 0.0)
    first = lax.broadcasted_iota(jnp.int32, (16, count), 0) == 0
    owned = lax.dot_general(
        jnp.where(first, owned, 0.0).astype(bf16), jnp.ones((16, columns), bf16),
        (((0,), (0,)), ((), ())), preferred_element_type=f32,
    )
    own_rows[...] = jnp.where(owned > 0.5, own_ref[...], 0.0)
    lines = lax.broadcasted_iota(jnp.int32, (columns, LANES), 0) + col_offset
    onehot = jnp.where(lines == line_ref[0:1, :], 1.0, 0.0)
    square_part[...] = jnp.dot(own_rows[...], onehot, precision=HIGHEST, preferred_element_type=f32)

    enter(core, partner, axes)
    x, y, z = axes["x"][0], axes["y"][0], axes["z"][0]
    for slot, peer, side in around(axes["z"][0]):
        lines = pl.ds(aligned((side * 4 + peer) * quarter, 8), quarter)
        send(square_part.at[lines], z_rx.at[slot], 0, 0, axes["z"][1](peer, side))
    panel_piece = count // 4
    scatter("x", own_rows, 0, panel_piece, panel_rx, 1, 0)
    loads[0].wait()
    weight_part[...] = jnp.dot(weight_ref[...], onehot.astype(bf16), preferred_element_type=f32).astype(bf16)
    send(weight_part.at[pl.ds(aligned((1 - core) * share, 16), share)], weight_rx, 2, 1, partner)
    arrive(weight_rx, 2)
    weight_half[...] = weight_part[pl.ds(aligned(core * share, 16), share), :] + weight_rx[...]
    span = share // 2
    piece = span // 4
    small = piece // 4
    scatter("y", weight_half, 0, piece, first_rx.at[0], 6, 1)
    scatter("z", weight_half, span, piece, first_rx.at[1], 7, 1)

    loads[2].wait()
    limits[...] = jnp.broadcast_to(limit_ref[0:1, :].astype(f32), limits.shape).astype(bf16)
    place_line = lax.broadcasted_iota(jnp.int32, (BLK, columns), 0)
    block = lax.axis_index("cols") * blocks + lax.broadcasted_iota(jnp.int32, (BLK, columns), 1) // BLK
    before = jnp.where(place_line <= block, 1.0, 0.0).astype(bf16)
    here = jnp.where(place_line == block, 1.0, 0.0).astype(bf16)
    lead = jnp.where(lax.broadcasted_iota(jnp.int32, (16, columns), 0) == 0, 1.0, 0.0).astype(bf16)

    def keep(low_chunk, high_chunk):
        @pl.loop(low_chunk, high_chunk)
        def _(i):
            spots = pl.ds(aligned(i * chunk, chunk), chunk)
            mask = mask_ref[spots, :].astype(f32).astype(bf16)
            seen = jnp.dot(mask, before, preferred_element_type=f32)
            bit = jnp.dot(mask, here, preferred_element_type=f32)
            limit = lax.dot_general(
                limits[:, spots], lead, (((0,), (0,)), ((), ())), preferred_element_type=f32
            )
            kept[spots, :] = jnp.where(seen <= limit, bit, 0.0).astype(bf16)

    arrive(z_rx, 0)
    mine = pl.ds(aligned((core * 4 + z) * quarter, 8), quarter)
    z_sum[...] = total(square_part[mine, :], z_rx) + total(z_rx[3], z_rx.at[pl.ds(4, 3)])
    spread("y", z_sum, lambda slot: y_rx.at[slot], 4, 0)
    keep(0, chunks)
    arrive(y_rx, 4)
    y_sum[...] = total(z_sum[...], y_rx)
    spread("x", y_sum, lambda slot: x_rx.at[slot], 5, 0)
    arrive(first_rx.at[0], 6)
    first_sum[0] = total(weight_half[pl.ds(aligned(y * piece, 16), piece), :], first_rx.at[0])
    scatter("z", first_sum.at[0], 0, small, second_rx.at[0], 11, 1)
    arrive(first_rx.at[1], 7)
    first_sum[1] = total(weight_half[pl.ds(aligned(span + z * piece, 16), piece), :], first_rx.at[1])
    scatter("y", first_sum.at[1], 0, small, second_rx.at[1], 12, 1)
    arrive(x_rx, 5)
    square_ref[mine, :] = total(y_sum[...], x_rx)
    for slot, peer, side in around(z):
        send(square_ref.at[mine], square_ref.at[mine], 8, 0, axes["z"][1](peer, side))
    arrive(panel_rx, 1)
    own_panel = pl.ds(aligned(x * panel_piece, 8), panel_piece)
    panel_ref[own_panel, :] = total(own_rows[own_panel, :], panel_rx)
    spread("x", panel_ref.at[own_panel], lambda slot: panel_ref.at[own_panel], 9, 0)
    arrive(second_rx.at[0], 11)
    base_a = core * share + y * piece
    base_b = core * share + span + z * piece
    slice_a = pl.ds(aligned(base_a + z * small, 16), small)
    slice_b = pl.ds(aligned(base_b + y * small, 16), small)
    chosen_ref[slice_a, :] = total(first_sum[0, pl.ds(aligned(z * small, 16), small), :], second_rx.at[0])
    spread("z", chosen_ref.at[slice_a], lambda slot: chosen_ref.at[slice_a], 13, 1)
    arrive(second_rx.at[1], 12)
    chosen_ref[slice_b, :] = total(first_sum[1, pl.ds(aligned(y * small, 16), small), :], second_rx.at[1])
    spread("y", chosen_ref.at[slice_b], lambda slot: chosen_ref.at[slice_b], 14, 1)
    loads[1].wait()
    send(features_ref, features_rx, 18, 2, partner)
    keep(chunks, 2 * chunks)
    arrive(chosen_ref.at[pl.ds(0, 3 * small)], 13)
    piece_a = pl.ds(aligned(base_a, 16), piece)
    spread("y", chosen_ref.at[piece_a], lambda slot: chosen_ref.at[piece_a], 15, 1)
    arrive(chosen_ref.at[pl.ds(0, 3 * small)], 14)
    piece_b = pl.ds(aligned(base_b, 16), piece)
    spread("z", chosen_ref.at[piece_b], lambda slot: chosen_ref.at[piece_b], 16, 1)
    arrive(square_ref.at[pl.ds(0, 7 * quarter)], 8)
    own_share = pl.ds(aligned(core * share, 16), share)

    def between(t):
        @pl.when(t == 1)
        def _():
            arrive(chosen_ref.at[pl.ds(0, 3 * piece)], 15)
            arrive(chosen_ref.at[pl.ds(0, 3 * piece)], 16)
            send(chosen_ref.at[own_share], chosen_ref.at[own_share], 17, 1, partner)

    state[...] = square_ref[...]
    invert(state, right, between)
    arrive(panel_ref.at[pl.ds(0, 3 * panel_piece)], 9)
    coeffs = jnp.dot(state[:, :count], panel_ref[...], precision=HIGHEST, preferred_element_type=f32)
    high[...] = coeffs.astype(bf16)
    low[...] = (coeffs - high[...].astype(f32)).astype(bf16)
    arrive(chosen_ref.at[pl.ds(0, share)], 17)

    def pruned_copy(i):
        spots = pl.ds(aligned(i * chunk, chunk), chunk)
        return pltpu.make_async_copy(pruned_ref.at[spots], pruned_any.at[spots], pruned_sem)

    def differ(index):
        spots = pl.ds(aligned(index * chunk, chunk), chunk)
        chosen = chosen_ref[spots, :][:, :count]
        change = jnp.dot(chosen, high[...], preferred_element_type=f32)
        change += jnp.dot(chosen, low[...], preferred_element_type=f32)
        wide = weight_ref[spots, :].astype(f32)
        masked = (wide - change) * kept[spots, :].astype(f32)
        pruned_ref[spots, :] = masked.astype(bf16)
        return (wide - masked).astype(bf16)

    def prepare(k):
        spots = slice(k * chunk, (k + 1) * chunk)
        sent_diff[spots, :] = differ((1 - core) * chunks + k)
        send(sent_diff.at[spots], diff_rx.at[spots], 20 + k, 2, partner)
        own_diff[spots, :] = differ(core * chunks + k)

    token_blocks = part.shape[1]

    def multiply(k):
        spots = slice(k * chunk, (k + 1) * chunk)
        tokens = features_ref.shape[0] // token_blocks

        @pl.loop(0, token_blocks)
        def _(t):
            words = pl.ds(aligned(t * tokens, tokens), tokens)
            product = lax.dot_general(
                features_ref[words, :], own_diff[spots, :], (((1,), (1,)), ((), ())), preferred_element_type=f32
            )
            product += lax.dot_general(
                features_rx[words, :], diff_rx[spots, :], (((1,), (1,)), ((), ())), preferred_element_type=f32
            )
            part[k, t] = product.astype(bf16).reshape(part.shape[2:])

    def ring(axis, parcel, value, extent, through_rx, through, rx, first):
        index, device = axes[axis]
        right_one, left_one, across = lax.rem(index + 1, 4), lax.rem(index + 3, 4), lax.rem(index + 2, 4)
        lo, hi = pl.ds(0, extent // 2), pl.ds(extent // 2, extent // 2)
        send(parcel(across).at[lo], through_rx.at[0], first, 3, device(right_one))
        send(parcel(across).at[hi], through_rx.at[1], first + 1, 3, device(left_one))
        send(parcel(right_one).at[hi], rx.at[0, hi], first + 2, 3, device(right_one))
        send(parcel(left_one).at[lo], rx.at[1, lo], first + 2, 3, device(left_one))

        def pass_on():
            arrive(through_rx.at[0], first)
            through[0] = (value(right_one, lo) + through_rx[0].astype(f32)).astype(bf16)
            send(through.at[0], rx.at[0, lo], first + 2, 3, device(right_one))
            arrive(through_rx.at[1], first + 1)
            through[1] = (value(left_one, hi) + through_rx[1].astype(f32)).astype(bf16)
            send(through.at[1], rx.at[1, hi], first + 2, 3, device(left_one))

        def finish():
            arrive(rx, first + 2)
            return value(index, pl.ds(0, extent)) + rx[0].astype(f32) + rx[1].astype(f32)

        return pass_on, finish

    order = [k for pair in zip(range(chunks // 2), range(chunks // 2, chunks)) for k in pair]
    rings = {}

    def reduce_first(k):
        if k == order[0]:
            arrive(features_rx, 18)
        arrive(diff_rx.at[k * chunk : (k + 1) * chunk], 20 + k)
        multiply(k)
        if k < chunks // 2:
            axis = "y"
            parcel = functools.partial(lambda k, j: part.at[k, j], k)
        else:
            axis = "z"
            parcel = functools.partial(lambda k, j: part.at[k, :, j], k)
        value = functools.partial(lambda parcel, j, which: parcel(j).at[which][...].astype(f32), parcel)
        rings[k] = ring(axis, parcel, value, 4, forward_rx.at[k], forward.at[k], ring_rx.at[k], 24 + 3 * k)

    prepare(order[0])
    prepare(order[1])
    for n, k in enumerate(order):
        reduce_first(k)
        if n + 2 < chunks:
            prepare(order[n + 2])
    for k in range(2 * chunks):
        pruned_copy(k).start()
    for k in order:
        rings[k][0]()
    tokens = error_ref.shape[0]
    for k in order:
        value_sum = rings[k][1]()
        sums_wide[k] = value_sum
        sums[k] = value_sum.astype(bf16)
        index, device = axes["z" if k < chunks // 2 else "y"]
        for slot, peer, side in around(index):
            words = pl.ds(aligned(side * tokens, tokens), tokens)
            send(sums.at[k, peer, words], last_rx.at[k, slot], 24 + 3 * chunks + k, 3, device(peer, side))
    for k in order:
        index = axes["z" if k < chunks // 2 else "y"][0]
        arrive(last_rx.at[k], 24 + 3 * chunks + k)
        here_sum = sums_wide[k, index, pl.ds(aligned(core * tokens, tokens), tokens), :]
        there_sum = last_rx[k, 0].astype(f32)
        for step in (1, 2, 3):
            here_sum += last_rx[k, 2 * step - 1].astype(f32)
            there_sum += last_rx[k, 2 * step].astype(f32)
        error_ref[:, pl.ds(aligned(core * share + k * chunk, chunk), chunk)] = here_sum
        error_ref[:, pl.ds(aligned((1 - core) * share + k * chunk, chunk), chunk)] = there_sum
    pltpu.make_async_copy(pruned_ref, pruned_any, pruned_sem).wait()
    unit_bytes = columns * jnp.dtype(weight_ref.dtype).itemsize
    for group, size in sent.items():
        view = weight_ref.at[pl.ds(0, size // unit_bytes)]
        remote(view, view, 0, group, partner).wait_send()


def prune(own_rows, line, limit, weight, mask, features, height):
    count, columns = own_rows.shape
    rows = weight.shape[0]
    tokens = features.shape[0]
    f32, bf16 = jnp.float32, jnp.bfloat16
    quarter = count // 8
    share, chunks = rows // 2, 4
    piece = share // 8
    small = piece // 4
    chunk = share // chunks
    vmem = pl.BlockSpec(memory_space=pltpu.VMEM)
    hbm = pl.BlockSpec(memory_space=pl.ANY)
    arrivals = 24 + 4 * chunks
    return pl.pallas_call(
        functools.partial(prune_kernel, height=height),
        out_shape=(
            jax.ShapeDtypeStruct((rows, columns), bf16),
            jax.ShapeDtypeStruct((tokens // 32, rows), f32),
        ),
        in_specs=[vmem, vmem, vmem, hbm, hbm, hbm],
        out_specs=(hbm, vmem),
        scratch_shapes=[
            pltpu.VMEM((rows, columns), bf16),
            pltpu.VMEM(mask.shape, jnp.int32),
            pltpu.VMEM(features.shape, bf16),
            pltpu.VMEM((rows, columns), bf16),
            pltpu.VMEM((16, rows), bf16),
            pltpu.VMEM((count, columns), f32),
            pltpu.VMEM((count, LANES), f32),
            pltpu.VMEM((7, quarter, LANES), f32),
            pltpu.VMEM((quarter, LANES), f32),
            pltpu.VMEM((3, quarter, LANES), f32),
            pltpu.VMEM((quarter, LANES), f32),
            pltpu.VMEM((3, quarter, LANES), f32),
            pltpu.VMEM((count, LANES), f32),
            pltpu.VMEM((count, LANES), f32),
            pltpu.VMEM((BLK, LANES), f32),
            pltpu.VMEM((3, count // 4, columns), f32),
            pltpu.VMEM((count, columns), f32),
            pltpu.VMEM((rows, LANES), bf16),
            pltpu.VMEM((share, LANES), bf16),
            pltpu.VMEM((share, LANES), bf16),
            pltpu.VMEM((2, 3, piece, LANES), bf16),
            pltpu.VMEM((2, piece, LANES), bf16),
            pltpu.VMEM((2, 3, small, LANES), bf16),
            pltpu.VMEM((rows, LANES), bf16),
            pltpu.VMEM((count, columns), bf16),
            pltpu.VMEM((count, columns), bf16),
            pltpu.VMEM(features.shape, bf16),
            pltpu.VMEM((share, columns), bf16),
            pltpu.VMEM((share, columns), bf16),
            pltpu.VMEM((share, columns), bf16),
            pltpu.VMEM((rows, columns), bf16),
            pltpu.VMEM((chunks, 4, 4, 64, chunk), bf16),
            pltpu.VMEM((chunks, 2, 2, 64, chunk), bf16),
            pltpu.VMEM((chunks, 2, 2, 64, chunk), bf16),
            pltpu.VMEM((chunks, 2, 4, 64, chunk), bf16),
            pltpu.VMEM((chunks, 4, 64, chunk), bf16),
            pltpu.VMEM((chunks, 4, 64, chunk), f32),
            pltpu.VMEM((chunks, 7, tokens // 32, chunk), bf16),
            pltpu.SemaphoreType.DMA((4,)),
            pltpu.SemaphoreType.DMA((arrivals,)),
            pltpu.SemaphoreType.DMA((3,)),
            pltpu.SemaphoreType.DMA,
        ],
        compiler_params=pltpu.CompilerParams(
            collective_id=0, has_side_effects=True, vmem_limit_bytes=56 << 20
        ),
        name="prune",
    )(own_rows, line, limit, weight, mask, features)


def local(weight, hess_inv, selected, block_mask, row_limits, calibration):
    rows_local = hess_inv.shape[0]
    row_offset = (lax.axis_index("rows") * rows_local).astype(jnp.int32).reshape(1)
    own_rows, line = gather(row_offset, selected, hess_inv)
    pruned, error = prune(
        own_rows, line, row_limits.reshape(1, -1), weight, block_mask, calibration, rows_local
    )
    return (pruned, error.T)


def solution(mesh):
    placed = (
        P("rows", "cols"),
        P("rows", "cols"),
        P(),
        P("rows", None),
        P("rows"),
        P(None, "cols"),
    )
    return jax.shard_map(
        local,
        mesh=mesh,
        in_specs=placed,
        out_specs=(P("rows", "cols"), P("rows", "cols")),
        check_vma=False,
    )
```

```python
import functools

import jax
import jax.numpy as jnp
from jax import lax
from jax.experimental import pallas as pl
from jax.experimental.pallas import tpu as pltpu
from jax.sharding import PartitionSpec as P

BLK = 128
LANES = 256
MESH = pl.DeviceIdType.MESH
HIGHEST = lax.Precision.HIGHEST


def aligned(value, factor):
    return pl.multiple_of(value, factor)


def place():
    row = lax.axis_index("rows")
    col = lax.axis_index("cols")
    core = lax.rem(col, 2)
    z = lax.rem(col // 2, 4)
    y = col // 8
    partner = (row, col + 1 - 2 * core)
    axes = {
        "x": (row, lambda j, k=core: (j, (y * 4 + z) * 2 + k)),
        "y": (y, lambda j, k=core: (row, (j * 4 + z) * 2 + k)),
        "z": (z, lambda j, k=core: (row, (y * 4 + j) * 2 + k)),
    }
    return core, partner, axes


def enter(core, partner, axes):
    barrier = pltpu.get_barrier_semaphore()
    greeted = [partner]
    for name, (index, device) in axes.items():
        for step in (1, 2, 3):
            peer = lax.rem(index + step, 4)
            greeted.append(device(peer))
            if name != "x":
                greeted.append(device(peer, 1 - core))
    for other in greeted:
        pl.semaphore_signal(barrier, inc=1, device_id=other, device_id_type=MESH)
    pl.semaphore_wait(barrier, len(greeted))


def gather_kernel(offset_ref, selected_ref, values_ref, inverse_ref, own_ref, line_ref, sem):
    steps, width = selected_ref.shape
    height = inverse_ref.shape[0]
    def row_copy(spot, k):
        return pltpu.make_async_copy(inverse_ref.at[pl.ds(spot, 1)], own_ref.at[pl.ds(k, 1)], sem)

    owned = 0
    for step in range(steps):

        def start(k, owned):
            spot = selected_ref[step, k] - offset_ref[0]
            inside = (spot >= 0) & (spot < height)

            @pl.when(inside)
            def _():
                row_copy(spot, step * width + k).start()

            return owned + jnp.where(inside, 1, 0)

        owned = lax.fori_loop(0, width, start, owned, unroll=8)
    line_ref[...] = jnp.full(line_ref.shape, -1, jnp.int32)
    for step in range(steps):
        line_ref[0:1, step * width : (step + 1) * width] = values_ref[step : step + 1, :]

    def finish(k, carry):
        row_copy(0, 0).wait()
        return carry

    lax.fori_loop(0, owned, finish, 0)


def gather(offset, selected, inverse):
    count = selected.size
    smem = pl.BlockSpec(memory_space=pltpu.SMEM)
    vmem = pl.BlockSpec(memory_space=pltpu.VMEM)
    return pl.pallas_call(
        gather_kernel,
        out_shape=(
            jax.ShapeDtypeStruct((count, inverse.shape[1]), jnp.float32),
            jax.ShapeDtypeStruct((8, LANES), jnp.int32),
        ),
        in_specs=[smem, smem, vmem, pl.BlockSpec(memory_space=pl.ANY)],
        out_specs=(vmem, vmem),
        scratch_shapes=[pltpu.SemaphoreType.DMA],
        name="gather",
    )(offset, selected, selected, inverse)


def invert(state, right, between):
    count, width = state.shape
    size, side = 8, 64
    blocks = side // size
    lane = lax.broadcasted_iota(jnp.int32, (size, BLK), 1)
    line = lax.broadcasted_iota(jnp.int32, (size, BLK), 0)

    def column(tile, at):
        picked = jnp.where(lane == at, tile, 0.0)
        return jnp.broadcast_to(jnp.sum(picked, axis=1, keepdims=True), tile.shape)

    def row(tile, k):
        return jnp.broadcast_to(tile[k : k + 1, :], tile.shape)

    def fold(parts):
        while len(parts) > 1:
            parts = [parts[i] + parts[i + 1] for i in range(0, len(parts), 2)]
        return parts[0]

    def step(t, carry):
        half = t // 2
        shift = (t - half * 2) * side
        lanes = pl.ds(aligned(half * BLK, BLK), BLK)
        groups = [state[pl.ds(aligned(t * side + i * size, size), size), lanes] for i in range(blocks)]
        for b in range(blocks):
            at = shift + b * size
            pivot = [column(groups[b], at + j) for j in range(size)]
            for k in range(size):
                scale = 1.0 / row(pivot[k], k)
                lead = pivot[k]
                for j in range(size):
                    if j != k:
                        scaled = row(pivot[j], k) * scale
                        pivot[j] = jnp.where(line == k, scaled, pivot[j] - lead * scaled)
                pivot[k] = jnp.where(line == k, scale, -lead * scale)
            inside = (lane >= at) & (lane < at + size)
            tile = jnp.where(inside, jnp.where(lane - at == line, 1.0, 0.0), groups[b])
            fresh = fold([pivot[j] * row(tile, j) for j in range(size)])
            rows = [row(fresh, j) for j in range(size)]
            order = [(b + 1 + i) % blocks for i in range(blocks - 1)]
            for i in order:
                change = fold([column(groups[i], at + j) * rows[j] for j in range(size)])
                groups[i] = jnp.where(inside, 0.0, groups[i]) - change
            groups[b] = fresh
        mine = (lane >= shift) & (lane < shift + side)
        block = jnp.concatenate([jnp.where(mine, group, 0.0) for group in groups], axis=0)
        own = pl.ds(aligned(shift, side), side)
        lines = pl.ds(aligned(t * side, side), side)
        wide = lax.broadcasted_iota(jnp.int32, (side, width), 1) - t * side
        unit = jnp.where(wide == lax.broadcasted_iota(jnp.int32, (side, width), 0), 1.0, 0.0)
        right[...] = jnp.zeros(right.shape, jnp.float32)
        right[own, :] = jnp.where((wide >= 0) & (wide < side), unit, state[lines, :])
        solved = jnp.dot(block, right[...], precision=HIGHEST, preferred_element_type=jnp.float32)
        right[own, :] = solved
        tall = lax.broadcasted_iota(jnp.int32, (count, BLK), 1)
        strip = jnp.where((tall >= shift) & (tall < shift + side), state[:, lanes], 0.0)
        spans = lax.broadcasted_iota(jnp.int32, (count, width), 1) - t * side
        cleared = jnp.where((spans >= 0) & (spans < side), 0.0, state[...])
        state[...] = cleared - jnp.dot(strip, right[...], precision=HIGHEST, preferred_element_type=jnp.float32)
        state[lines, :] = solved
        between(t)
        return carry

    lax.fori_loop(0, count // side, step, 0)


def prune_kernel(
    own_ref, line_ref, limit_ref, weight_any, mask_any, features_any, pruned_ref, error_ref,
    weight_ref, mask_ref, features_ref, kept, limits,
    own_rows, square_part, z_rx, z_sum, y_rx, y_sum, x_rx, square_ref, state, right,
    panel_rx, panel_ref, weight_part, weight_rx, weight_half, first_rx, first_sum, second_rx, chosen_ref,
    high, low, features_rx, own_diff, sent_diff, diff_rx, part, forward_rx, forward, ring_rx,
    sums, sums_wide, last_rx,
    send_sem, recv_sem, local_sem,
    *, height,
):
    core, partner, axes = place()
    rows, columns = weight_ref.shape
    col_offset = lax.axis_index("cols") * columns
    count = own_ref.shape[0]
    quarter = count // 8
    share = rows // 2
    chunks = part.shape[0]
    chunk = share // chunks
    blocks = columns // BLK
    f32, bf16 = jnp.float32, jnp.bfloat16
    loads = [
        pltpu.make_async_copy(src, dst, local_sem.at[i])
        for i, (src, dst) in enumerate(
            ((weight_any, weight_ref), (features_any, features_ref), (mask_any, mask_ref))
        )
    ]
    for load in loads:
        load.start()

    sent = {}

    def remote(src, dst, arrival, group, device):
        return pltpu.make_async_remote_copy(
            src_ref=src, dst_ref=dst, send_sem=send_sem.at[group], recv_sem=recv_sem.at[arrival],
            device_id=device, device_id_type=MESH,
        )

    def send(src, dst, arrival, group, device):
        remote(src, dst, arrival, group, device).start()
        size = jnp.dtype(src.dtype).itemsize
        for extent in src.shape:
            size *= extent
        sent[group] = sent.get(group, 0) + size

    def arrive(view, arrival):
        remote(view, view, arrival, 0, partner).wait_recv()

    def scatter(axis, src, base, piece, rx, arrival, group):
        index, device = axes[axis]
        for step in (1, 2, 3):
            peer = lax.rem(index + step, 4)
            start = aligned(base + peer * piece, 8)
            send(src.at[pl.ds(start, piece)], rx.at[step - 1], arrival, group, device(peer))

    def spread(axis, src, dst_of, arrival, group):
        index, device = axes[axis]
        for step in (1, 2, 3):
            send(src, dst_of(step - 1), arrival, group, device(lax.rem(index + step, 4)))

    def around(index):
        for step in range(4):
            for turn in range(2):
                if step + turn > 0:
                    yield 2 * step + turn - 1, lax.rem(index + step, 4), lax.rem(core + turn, 2)

    def total(own, rx):
        return own + rx[0] + rx[1] + rx[2]

    row_offset = lax.axis_index("rows") * height
    picked = line_ref[0:1, :count]
    owned = jnp.where((picked >= row_offset) & (picked < row_offset + height), 1.0, 0.0)
    first = lax.broadcasted_iota(jnp.int32, (16, count), 0) == 0
    owned = lax.dot_general(
        jnp.where(first, owned, 0.0).astype(bf16), jnp.ones((16, columns), bf16),
        (((0,), (0,)), ((), ())), preferred_element_type=f32,
    )
    own_rows[...] = jnp.where(owned > 0.5, own_ref[...], 0.0)
    lines = lax.broadcasted_iota(jnp.int32, (columns, LANES), 0) + col_offset
    onehot = jnp.where(lines == line_ref[0:1, :], 1.0, 0.0)
    square_part[...] = jnp.dot(own_rows[...], onehot, precision=HIGHEST, preferred_element_type=f32)

    enter(core, partner, axes)
    x, y, z = axes["x"][0], axes["y"][0], axes["z"][0]
    for slot, peer, side in around(axes["z"][0]):
        lines = pl.ds(aligned((side * 4 + peer) * quarter, 8), quarter)
        send(square_part.at[lines], z_rx.at[slot], 0, 0, axes["z"][1](peer, side))
    panel_piece = count // 4
    scatter("x", own_rows, 0, panel_piece, panel_rx, 1, 0)
    loads[0].wait()
    weight_part[...] = jnp.dot(weight_ref[...], onehot.astype(bf16), preferred_element_type=f32).astype(bf16)
    send(weight_part.at[pl.ds(aligned((1 - core) * share, 16), share)], weight_rx, 2, 1, partner)
    arrive(weight_rx, 2)
    weight_half[...] = weight_part[pl.ds(aligned(core * share, 16), share), :] + weight_rx[...]
    span = share // 2
    piece = span // 4
    small = piece // 4
    scatter("y", weight_half, 0, piece, first_rx.at[0], 6, 1)
    scatter("z", weight_half, span, piece, first_rx.at[1], 7, 1)

    loads[2].wait()
    limits[...] = jnp.broadcast_to(limit_ref[0:1, :].astype(f32), limits.shape).astype(bf16)
    place_line = lax.broadcasted_iota(jnp.int32, (BLK, columns), 0)
    block = lax.axis_index("cols") * blocks + lax.broadcasted_iota(jnp.int32, (BLK, columns), 1) // BLK
    before = jnp.where(place_line <= block, 1.0, 0.0).astype(bf16)
    here = jnp.where(place_line == block, 1.0, 0.0).astype(bf16)
    lead = jnp.where(lax.broadcasted_iota(jnp.int32, (16, columns), 0) == 0, 1.0, 0.0).astype(bf16)

    def keep(low_chunk, high_chunk):
        @pl.loop(low_chunk, high_chunk)
        def _(i):
            spots = pl.ds(aligned(i * chunk, chunk), chunk)
            mask = mask_ref[spots, :].astype(f32).astype(bf16)
            seen = jnp.dot(mask, before, preferred_element_type=f32)
            bit = jnp.dot(mask, here, preferred_element_type=f32)
            limit = lax.dot_general(
                limits[:, spots], lead, (((0,), (0,)), ((), ())), preferred_element_type=f32
            )
            kept[spots, :] = jnp.where(seen <= limit, bit, 0.0).astype(bf16)

    arrive(z_rx, 0)
    mine = pl.ds(aligned((core * 4 + z) * quarter, 8), quarter)
    z_sum[...] = total(square_part[mine, :], z_rx) + total(z_rx[3], z_rx.at[pl.ds(4, 3)])
    spread("y", z_sum, lambda slot: y_rx.at[slot], 4, 0)
    keep(0, chunks)
    arrive(y_rx, 4)
    y_sum[...] = total(z_sum[...], y_rx)
    spread("x", y_sum, lambda slot: x_rx.at[slot], 5, 0)
    arrive(first_rx.at[0], 6)
    first_sum[0] = total(weight_half[pl.ds(aligned(y * piece, 16), piece), :], first_rx.at[0])
    scatter("z", first_sum.at[0], 0, small, second_rx.at[0], 11, 1)
    arrive(first_rx.at[1], 7)
    first_sum[1] = total(weight_half[pl.ds(aligned(span + z * piece, 16), piece), :], first_rx.at[1])
    scatter("y", first_sum.at[1], 0, small, second_rx.at[1], 12, 1)
    arrive(x_rx, 5)
    square_ref[mine, :] = total(y_sum[...], x_rx)
    for slot, peer, side in around(z):
        send(square_ref.at[mine], square_ref.at[mine], 8, 0, axes["z"][1](peer, side))
    arrive(panel_rx, 1)
    own_panel = pl.ds(aligned(x * panel_piece, 8), panel_piece)
    panel_ref[own_panel, :] = total(own_rows[own_panel, :], panel_rx)
    spread("x", panel_ref.at[own_panel], lambda slot: panel_ref.at[own_panel], 9, 0)
    arrive(second_rx.at[0], 11)
    base_a = core * share + y * piece
    base_b = core * share + span + z * piece
    slice_a = pl.ds(aligned(base_a + z * small, 16), small)
    slice_b = pl.ds(aligned(base_b + y * small, 16), small)
    chosen_ref[slice_a, :] = total(first_sum[0, pl.ds(aligned(z * small, 16), small), :], second_rx.at[0])
    spread("z", chosen_ref.at[slice_a], lambda slot: chosen_ref.at[slice_a], 13, 1)
    arrive(second_rx.at[1], 12)
    chosen_ref[slice_b, :] = total(first_sum[1, pl.ds(aligned(y * small, 16), small), :], second_rx.at[1])
    spread("y", chosen_ref.at[slice_b], lambda slot: chosen_ref.at[slice_b], 14, 1)
    loads[1].wait()
    send(features_ref, features_rx, 18, 2, partner)
    keep(chunks, 2 * chunks)
    arrive(chosen_ref.at[pl.ds(0, 3 * small)], 13)
    piece_a = pl.ds(aligned(base_a, 16), piece)
    spread("y", chosen_ref.at[piece_a], lambda slot: chosen_ref.at[piece_a], 15, 1)
    arrive(chosen_ref.at[pl.ds(0, 3 * small)], 14)
    piece_b = pl.ds(aligned(base_b, 16), piece)
    spread("z", chosen_ref.at[piece_b], lambda slot: chosen_ref.at[piece_b], 16, 1)
    arrive(square_ref.at[pl.ds(0, 7 * quarter)], 8)
    own_share = pl.ds(aligned(core * share, 16), share)

    def between(t):
        @pl.when(t == 1)
        def _():
            arrive(chosen_ref.at[pl.ds(0, 3 * piece)], 15)
            arrive(chosen_ref.at[pl.ds(0, 3 * piece)], 16)
            send(chosen_ref.at[own_share], chosen_ref.at[own_share], 17, 1, partner)

    state[...] = square_ref[...]
    invert(state, right, between)
    arrive(panel_ref.at[pl.ds(0, 3 * panel_piece)], 9)
    coeffs = jnp.dot(state[:, :count], panel_ref[...], precision=HIGHEST, preferred_element_type=f32)
    high[...] = coeffs.astype(bf16)
    low[...] = (coeffs - high[...].astype(f32)).astype(bf16)
    arrive(chosen_ref.at[pl.ds(0, share)], 17)

    def differ(index):
        spots = pl.ds(aligned(index * chunk, chunk), chunk)
        chosen = chosen_ref[spots, :][:, :count]
        change = jnp.dot(chosen, high[...], preferred_element_type=f32)
        change += jnp.dot(chosen, low[...], preferred_element_type=f32)
        wide = weight_ref[spots, :].astype(f32)
        masked = (wide - change) * kept[spots, :].astype(f32)
        pruned_ref[spots, :] = masked.astype(bf16)
        return (wide - masked).astype(bf16)

    def prepare_sent(k):
        spots = slice(k * chunk, (k + 1) * chunk)
        sent_diff[spots, :] = differ((1 - core) * chunks + k)
        send(sent_diff.at[spots], diff_rx.at[spots], 20 + k, 2, partner)

    def prepare_own(k):
        own_diff[k * chunk : (k + 1) * chunk, :] = differ(core * chunks + k)

    token_blocks = part.shape[1]

    def multiply(k):
        spots = slice(k * chunk, (k + 1) * chunk)
        tokens = features_ref.shape[0] // token_blocks

        @pl.loop(0, token_blocks)
        def _(t):
            words = pl.ds(aligned(t * tokens, tokens), tokens)
            product = lax.dot_general(
                features_ref[words, :], own_diff[spots, :], (((1,), (1,)), ((), ())), preferred_element_type=f32
            )
            product += lax.dot_general(
                features_rx[words, :], diff_rx[spots, :], (((1,), (1,)), ((), ())), preferred_element_type=f32
            )
            part[k, t] = product.astype(bf16).reshape(part.shape[2:])

    def ring(axis, parcel, value, extent, through_rx, through, rx, first):
        index, device = axes[axis]
        right_one, left_one, across = lax.rem(index + 1, 4), lax.rem(index + 3, 4), lax.rem(index + 2, 4)
        lo, hi = pl.ds(0, extent // 2), pl.ds(extent // 2, extent // 2)
        send(parcel(across).at[lo], through_rx.at[0], first, 3, device(right_one))
        send(parcel(across).at[hi], through_rx.at[1], first + 1, 3, device(left_one))
        send(parcel(right_one).at[hi], rx.at[0, hi], first + 2, 3, device(right_one))
        send(parcel(left_one).at[lo], rx.at[1, lo], first + 2, 3, device(left_one))

        def pass_on():
            arrive(through_rx.at[0], first)
            through[0] = (value(right_one, lo) + through_rx[0].astype(f32)).astype(bf16)
            send(through.at[0], rx.at[0, lo], first + 2, 3, device(right_one))
            arrive(through_rx.at[1], first + 1)
            through[1] = (value(left_one, hi) + through_rx[1].astype(f32)).astype(bf16)
            send(through.at[1], rx.at[1, hi], first + 2, 3, device(left_one))

        def finish():
            arrive(rx, first + 2)
            return value(index, pl.ds(0, extent)) + rx[0].astype(f32) + rx[1].astype(f32)

        return pass_on, finish

    order = [k for pair in zip(range(chunks // 2), range(chunks // 2, chunks)) for k in pair]
    rings = {}

    def reduce_first(k):
        if k == order[0]:
            arrive(features_rx, 18)
        arrive(diff_rx.at[k * chunk : (k + 1) * chunk], 20 + k)
        multiply(k)
        if k < chunks // 2:
            axis = "y"
            parcel = functools.partial(lambda k, j: part.at[k, j], k)
        else:
            axis = "z"
            parcel = functools.partial(lambda k, j: part.at[k, :, j], k)
        value = functools.partial(lambda parcel, j, which: parcel(j).at[which][...].astype(f32), parcel)
        rings[k] = ring(axis, parcel, value, 4, forward_rx.at[k], forward.at[k], ring_rx.at[k], 24 + 3 * k)

    for k in order:
        prepare_sent(k)
    prepare_own(order[0])
    prepare_own(order[1])
    for n, k in enumerate(order):
        reduce_first(k)
        if n + 2 < chunks:
            prepare_own(order[n + 2])
    for k in order:
        rings[k][0]()
    tokens = error_ref.shape[0]
    for k in order:
        value_sum = rings[k][1]()
        sums_wide[k] = value_sum
        sums[k] = value_sum.astype(bf16)
        index, device = axes["z" if k < chunks // 2 else "y"]
        for slot, peer, side in around(index):
            words = pl.ds(aligned(side * tokens, tokens), tokens)
            send(sums.at[k, peer, words], last_rx.at[k, slot], 24 + 3 * chunks + k, 3, device(peer, side))
    for k in order:
        index = axes["z" if k < chunks // 2 else "y"][0]
        arrive(last_rx.at[k], 24 + 3 * chunks + k)
        here_sum = sums_wide[k, index, pl.ds(aligned(core * tokens, tokens), tokens), :]
        there_sum = last_rx[k, 0].astype(f32)
        for step in (1, 2, 3):
            here_sum += last_rx[k, 2 * step - 1].astype(f32)
            there_sum += last_rx[k, 2 * step].astype(f32)
        error_ref[:, pl.ds(aligned(core * share + k * chunk, chunk), chunk)] = here_sum
        error_ref[:, pl.ds(aligned((1 - core) * share + k * chunk, chunk), chunk)] = there_sum
    unit_bytes = columns * jnp.dtype(weight_ref.dtype).itemsize
    for group, size in sent.items():
        view = weight_ref.at[pl.ds(0, size // unit_bytes)]
        remote(view, view, 0, group, partner).wait_send()


def prune(own_rows, line, limit, weight, mask, features, height):
    count, columns = own_rows.shape
    rows = weight.shape[0]
    tokens = features.shape[0]
    f32, bf16 = jnp.float32, jnp.bfloat16
    quarter = count // 8
    share, chunks = rows // 2, 4
    piece = share // 8
    small = piece // 4
    chunk = share // chunks
    vmem = pl.BlockSpec(memory_space=pltpu.VMEM)
    hbm = pl.BlockSpec(memory_space=pltpu.HBM)
    arrivals = 24 + 4 * chunks
    return pl.pallas_call(
        functools.partial(prune_kernel, height=height),
        out_shape=(
            jax.ShapeDtypeStruct((rows, columns), bf16),
            jax.ShapeDtypeStruct((tokens // 32, rows), f32),
        ),
        in_specs=[vmem, vmem, vmem, hbm, hbm, hbm],
        out_specs=(vmem, vmem),
        scratch_shapes=[
            pltpu.VMEM((rows, columns), bf16),
            pltpu.VMEM(mask.shape, jnp.int32),
            pltpu.VMEM(features.shape, bf16),
            pltpu.VMEM((rows, columns), bf16),
            pltpu.VMEM((16, rows), bf16),
            pltpu.VMEM((count, columns), f32),
            pltpu.VMEM((count, LANES), f32),
            pltpu.VMEM((7, quarter, LANES), f32),
            pltpu.VMEM((quarter, LANES), f32),
            pltpu.VMEM((3, quarter, LANES), f32),
            pltpu.VMEM((quarter, LANES), f32),
            pltpu.VMEM((3, quarter, LANES), f32),
            pltpu.VMEM((count, LANES), f32),
            pltpu.VMEM((count, LANES), f32),
            pltpu.VMEM((BLK, LANES), f32),
            pltpu.VMEM((3, count // 4, columns), f32),
            pltpu.VMEM((count, columns), f32),
            pltpu.VMEM((rows, LANES), bf16),
            pltpu.VMEM((share, LANES), bf16),
            pltpu.VMEM((share, LANES), bf16),
            pltpu.VMEM((2, 3, piece, LANES), bf16),
            pltpu.VMEM((2, piece, LANES), bf16),
            pltpu.VMEM((2, 3, small, LANES), bf16),
            pltpu.VMEM((rows, LANES), bf16),
            pltpu.VMEM((count, columns), bf16),
            pltpu.VMEM((count, columns), bf16),
            pltpu.VMEM(features.shape, bf16),
            pltpu.VMEM((share, columns), bf16),
            pltpu.VMEM((share, columns), bf16),
            pltpu.VMEM((share, columns), bf16),
            pltpu.VMEM((chunks, 4, 4, 64, chunk), bf16),
            pltpu.VMEM((chunks, 2, 2, 64, chunk), bf16),
            pltpu.VMEM((chunks, 2, 2, 64, chunk), bf16),
            pltpu.VMEM((chunks, 2, 4, 64, chunk), bf16),
            pltpu.VMEM((chunks, 4, 64, chunk), bf16),
            pltpu.VMEM((chunks, 4, 64, chunk), f32),
            pltpu.VMEM((chunks, 7, tokens // 32, chunk), bf16),
            pltpu.SemaphoreType.DMA((4,)),
            pltpu.SemaphoreType.DMA((arrivals,)),
            pltpu.SemaphoreType.DMA((3,)),
        ],
        compiler_params=pltpu.CompilerParams(
            collective_id=0, has_side_effects=True, vmem_limit_bytes=32 << 20
        ),
        name="prune",
    )(own_rows, line, limit, weight, mask, features)


def local(weight, hess_inv, selected, block_mask, row_limits, calibration):
    rows_local = hess_inv.shape[0]
    row_offset = (lax.axis_index("rows") * rows_local).astype(jnp.int32).reshape(1)
    own_rows, line = gather(row_offset, selected, hess_inv)
    pruned, error = prune(
        own_rows, line, row_limits.reshape(1, -1), weight, block_mask, calibration, rows_local
    )
    return (pruned, error.T)


def solution(mesh):
    placed = (
        P("rows", "cols"),
        P("rows", "cols"),
        P(),
        P("rows", None),
        P("rows"),
        P(None, "cols"),
    )
    return jax.shard_map(
        local,
        mesh=mesh,
        in_specs=placed,
        out_specs=(P("rows", "cols"), P("rows", "cols")),
        check_vma=False,
    )
```

```python
import functools

import jax
import jax.numpy as jnp
from jax import lax
from jax.experimental import pallas as pl
from jax.experimental.pallas import tpu as pltpu
from jax.sharding import PartitionSpec as P

BLK = 128
LANES = 256
MESH = pl.DeviceIdType.MESH
HIGHEST = lax.Precision.HIGHEST


def aligned(value, factor):
    return pl.multiple_of(value, factor)


def place():
    row = lax.axis_index("rows")
    col = lax.axis_index("cols")
    core = lax.rem(col, 2)
    z = lax.rem(col // 2, 4)
    y = col // 8
    partner = (row, col + 1 - 2 * core)
    axes = {
        "x": (row, lambda j, k=core: (j, (y * 4 + z) * 2 + k)),
        "y": (y, lambda j, k=core: (row, (j * 4 + z) * 2 + k)),
        "z": (z, lambda j, k=core: (row, (y * 4 + j) * 2 + k)),
    }
    return core, partner, axes


def enter(core, partner, axes):
    barrier = pltpu.get_barrier_semaphore()
    greeted = [partner]
    for name, (index, device) in axes.items():
        for step in (1, 2, 3):
            peer = lax.rem(index + step, 4)
            greeted.append(device(peer))
            if name != "x":
                greeted.append(device(peer, 1 - core))
    for other in greeted:
        pl.semaphore_signal(barrier, inc=1, device_id=other, device_id_type=MESH)
    pl.semaphore_wait(barrier, len(greeted))


def gather_kernel(offset_ref, selected_ref, values_ref, inverse_ref, own_ref, line_ref, sem):
    steps, width = selected_ref.shape
    height = inverse_ref.shape[0]
    def row_copy(spot, k):
        return pltpu.make_async_copy(inverse_ref.at[pl.ds(spot, 1)], own_ref.at[pl.ds(k, 1)], sem)

    owned = 0
    for step in range(steps):

        def start(k, owned):
            spot = selected_ref[step, k] - offset_ref[0]
            inside = (spot >= 0) & (spot < height)

            @pl.when(inside)
            def _():
                row_copy(spot, step * width + k).start()

            return owned + jnp.where(inside, 1, 0)

        owned = lax.fori_loop(0, width, start, owned, unroll=8)
    line_ref[...] = jnp.full(line_ref.shape, -1, jnp.int32)
    for step in range(steps):
        line_ref[0:1, step * width : (step + 1) * width] = values_ref[step : step + 1, :]

    def finish(k, carry):
        row_copy(0, 0).wait()
        return carry

    lax.fori_loop(0, owned, finish, 0)


def gather(offset, selected, inverse):
    count = selected.size
    smem = pl.BlockSpec(memory_space=pltpu.SMEM)
    vmem = pl.BlockSpec(memory_space=pltpu.VMEM)
    return pl.pallas_call(
        gather_kernel,
        out_shape=(
            jax.ShapeDtypeStruct((count, inverse.shape[1]), jnp.float32),
            jax.ShapeDtypeStruct((8, LANES), jnp.int32),
        ),
        in_specs=[smem, smem, vmem, pl.BlockSpec(memory_space=pl.ANY)],
        out_specs=(vmem, vmem),
        scratch_shapes=[pltpu.SemaphoreType.DMA],
        name="gather",
    )(offset, selected, selected, inverse)


def invert(state, right, between):
    count, width = state.shape
    size, side = 8, 64
    blocks = side // size
    lane = lax.broadcasted_iota(jnp.int32, (size, BLK), 1)
    line = lax.broadcasted_iota(jnp.int32, (size, BLK), 0)

    def column(tile, at):
        picked = jnp.where(lane == at, tile, 0.0)
        return jnp.broadcast_to(jnp.sum(picked, axis=1, keepdims=True), tile.shape)

    def row(tile, k):
        return jnp.broadcast_to(tile[k : k + 1, :], tile.shape)

    def fold(parts):
        while len(parts) > 1:
            parts = [parts[i] + parts[i + 1] for i in range(0, len(parts), 2)]
        return parts[0]

    def step(t, carry):
        half = t // 2
        shift = (t - half * 2) * side
        lanes = pl.ds(aligned(half * BLK, BLK), BLK)
        groups = [state[pl.ds(aligned(t * side + i * size, size), size), lanes] for i in range(blocks)]
        for b in range(blocks):
            at = shift + b * size
            pivot = [column(groups[b], at + j) for j in range(size)]
            for k in range(size):
                scale = 1.0 / row(pivot[k], k)
                lead = pivot[k]
                for j in range(size):
                    if j != k:
                        scaled = row(pivot[j], k) * scale
                        pivot[j] = jnp.where(line == k, scaled, pivot[j] - lead * scaled)
                pivot[k] = jnp.where(line == k, scale, -lead * scale)
            inside = (lane >= at) & (lane < at + size)
            tile = jnp.where(inside, jnp.where(lane - at == line, 1.0, 0.0), groups[b])
            fresh = fold([pivot[j] * row(tile, j) for j in range(size)])
            rows = [row(fresh, j) for j in range(size)]
            order = [(b + 1 + i) % blocks for i in range(blocks - 1)]
            for i in order:
                change = fold([column(groups[i], at + j) * rows[j] for j in range(size)])
                groups[i] = jnp.where(inside, 0.0, groups[i]) - change
            groups[b] = fresh
        mine = (lane >= shift) & (lane < shift + side)
        block = jnp.concatenate([jnp.where(mine, group, 0.0) for group in groups], axis=0)
        own = pl.ds(aligned(shift, side), side)
        lines = pl.ds(aligned(t * side, side), side)
        wide = lax.broadcasted_iota(jnp.int32, (side, width), 1) - t * side
        unit = jnp.where(wide == lax.broadcasted_iota(jnp.int32, (side, width), 0), 1.0, 0.0)
        right[...] = jnp.zeros(right.shape, jnp.float32)
        right[own, :] = jnp.where((wide >= 0) & (wide < side), unit, state[lines, :])
        solved = jnp.dot(block, right[...], precision=HIGHEST, preferred_element_type=jnp.float32)
        right[own, :] = solved
        tall = lax.broadcasted_iota(jnp.int32, (count, BLK), 1)
        strip = jnp.where((tall >= shift) & (tall < shift + side), state[:, lanes], 0.0)
        spans = lax.broadcasted_iota(jnp.int32, (count, width), 1) - t * side
        cleared = jnp.where((spans >= 0) & (spans < side), 0.0, state[...])
        state[...] = cleared - jnp.dot(strip, right[...], precision=HIGHEST, preferred_element_type=jnp.float32)
        state[lines, :] = solved
        between(t)
        return carry

    lax.fori_loop(0, count // side, step, 0)


def prune_kernel(
    own_ref, line_ref, limit_ref, weight_ref, mask_ref, features_ref, pruned_ref, error_ref,
    kept, limits,
    own_rows, square_part, z_rx, z_sum, y_rx, y_sum, x_rx, square_ref, state, right,
    panel_rx, panel_ref, weight_part, weight_rx, weight_half, first_rx, first_sum, second_rx, chosen_ref,
    high, low, features_rx, own_diff, sent_diff, diff_rx, part, forward_rx, forward, ring_rx,
    sums, sums_wide, last_rx,
    send_sem, recv_sem,
    *, height,
):
    core, partner, axes = place()
    rows, columns = weight_ref.shape
    col_offset = lax.axis_index("cols") * columns
    count = own_ref.shape[0]
    quarter = count // 8
    share = rows // 2
    chunks = part.shape[0]
    chunk = share // chunks
    blocks = columns // BLK
    f32, bf16 = jnp.float32, jnp.bfloat16
    sent = {}

    def remote(src, dst, arrival, group, device):
        return pltpu.make_async_remote_copy(
            src_ref=src, dst_ref=dst, send_sem=send_sem.at[group], recv_sem=recv_sem.at[arrival],
            device_id=device, device_id_type=MESH,
        )

    def send(src, dst, arrival, group, device):
        remote(src, dst, arrival, group, device).start()
        size = jnp.dtype(src.dtype).itemsize
        for extent in src.shape:
            size *= extent
        sent[group] = sent.get(group, 0) + size

    def arrive(view, arrival):
        remote(view, view, arrival, 0, partner).wait_recv()

    def scatter(axis, src, base, piece, rx, arrival, group):
        index, device = axes[axis]
        for step in (1, 2, 3):
            peer = lax.rem(index + step, 4)
            start = aligned(base + peer * piece, 8)
            send(src.at[pl.ds(start, piece)], rx.at[step - 1], arrival, group, device(peer))

    def spread(axis, src, dst_of, arrival, group):
        index, device = axes[axis]
        for step in (1, 2, 3):
            send(src, dst_of(step - 1), arrival, group, device(lax.rem(index + step, 4)))

    def around(index):
        for step in range(4):
            for turn in range(2):
                if step + turn > 0:
                    yield 2 * step + turn - 1, lax.rem(index + step, 4), lax.rem(core + turn, 2)

    def total(own, rx):
        return own + rx[0] + rx[1] + rx[2]

    row_offset = lax.axis_index("rows") * height
    picked = line_ref[0:1, :count]
    owned = jnp.where((picked >= row_offset) & (picked < row_offset + height), 1.0, 0.0)
    first = lax.broadcasted_iota(jnp.int32, (16, count), 0) == 0
    owned = lax.dot_general(
        jnp.where(first, owned, 0.0).astype(bf16), jnp.ones((16, columns), bf16),
        (((0,), (0,)), ((), ())), preferred_element_type=f32,
    )
    own_rows[...] = jnp.where(owned > 0.5, own_ref[...], 0.0)
    lines = lax.broadcasted_iota(jnp.int32, (columns, LANES), 0) + col_offset
    onehot = jnp.where(lines == line_ref[0:1, :], 1.0, 0.0)
    square_part[...] = jnp.dot(own_rows[...], onehot, precision=HIGHEST, preferred_element_type=f32)

    enter(core, partner, axes)
    x, y, z = axes["x"][0], axes["y"][0], axes["z"][0]
    for slot, peer, side in around(axes["z"][0]):
        lines = pl.ds(aligned((side * 4 + peer) * quarter, 8), quarter)
        send(square_part.at[lines], z_rx.at[slot], 0, 0, axes["z"][1](peer, side))
    panel_piece = count // 4
    scatter("x", own_rows, 0, panel_piece, panel_rx, 1, 0)
    weight_part[...] = jnp.dot(weight_ref[...], onehot.astype(bf16), preferred_element_type=f32).astype(bf16)
    send(weight_part.at[pl.ds(aligned((1 - core) * share, 16), share)], weight_rx, 2, 1, partner)
    arrive(weight_rx, 2)
    weight_half[...] = weight_part[pl.ds(aligned(core * share, 16), share), :] + weight_rx[...]
    span = share // 2
    piece = span // 4
    small = piece // 4
    scatter("y", weight_half, 0, piece, first_rx.at[0], 6, 1)
    scatter("z", weight_half, span, piece, first_rx.at[1], 7, 1)

    limits[...] = jnp.broadcast_to(limit_ref[0:1, :].astype(f32), limits.shape).astype(bf16)
    place_line = lax.broadcasted_iota(jnp.int32, (BLK, columns), 0)
    block = lax.axis_index("cols") * blocks + lax.broadcasted_iota(jnp.int32, (BLK, columns), 1) // BLK
    before = jnp.where(place_line <= block, 1.0, 0.0).astype(bf16)
    here = jnp.where(place_line == block, 1.0, 0.0).astype(bf16)
    lead = jnp.where(lax.broadcasted_iota(jnp.int32, (16, columns), 0) == 0, 1.0, 0.0).astype(bf16)

    def keep(low_chunk, high_chunk):
        @pl.loop(low_chunk, high_chunk)
        def _(i):
            spots = pl.ds(aligned(i * chunk, chunk), chunk)
            mask = mask_ref[spots, :].astype(f32).astype(bf16)
            seen = jnp.dot(mask, before, preferred_element_type=f32)
            bit = jnp.dot(mask, here, preferred_element_type=f32)
            limit = lax.dot_general(
                limits[:, spots], lead, (((0,), (0,)), ((), ())), preferred_element_type=f32
            )
            kept[spots, :] = jnp.where(seen <= limit, bit, 0.0).astype(bf16)

    arrive(z_rx, 0)
    mine = pl.ds(aligned((core * 4 + z) * quarter, 8), quarter)
    z_sum[...] = total(square_part[mine, :], z_rx) + total(z_rx[3], z_rx.at[pl.ds(4, 3)])
    spread("y", z_sum, lambda slot: y_rx.at[slot], 4, 0)
    keep(0, chunks)
    arrive(y_rx, 4)
    y_sum[...] = total(z_sum[...], y_rx)
    spread("x", y_sum, lambda slot: x_rx.at[slot], 5, 0)
    arrive(first_rx.at[0], 6)
    first_sum[0] = total(weight_half[pl.ds(aligned(y * piece, 16), piece), :], first_rx.at[0])
    scatter("z", first_sum.at[0], 0, small, second_rx.at[0], 11, 1)
    arrive(first_rx.at[1], 7)
    first_sum[1] = total(weight_half[pl.ds(aligned(span + z * piece, 16), piece), :], first_rx.at[1])
    scatter("y", first_sum.at[1], 0, small, second_rx.at[1], 12, 1)
    arrive(x_rx, 5)
    square_ref[mine, :] = total(y_sum[...], x_rx)
    for slot, peer, side in around(z):
        send(square_ref.at[mine], square_ref.at[mine], 8, 0, axes["z"][1](peer, side))
    arrive(panel_rx, 1)
    own_panel = pl.ds(aligned(x * panel_piece, 8), panel_piece)
    panel_ref[own_panel, :] = total(own_rows[own_panel, :], panel_rx)
    spread("x", panel_ref.at[own_panel], lambda slot: panel_ref.at[own_panel], 9, 0)
    arrive(second_rx.at[0], 11)
    base_a = core * share + y * piece
    base_b = core * share + span + z * piece
    slice_a = pl.ds(aligned(base_a + z * small, 16), small)
    slice_b = pl.ds(aligned(base_b + y * small, 16), small)
    chosen_ref[slice_a, :] = total(first_sum[0, pl.ds(aligned(z * small, 16), small), :], second_rx.at[0])
    spread("z", chosen_ref.at[slice_a], lambda slot: chosen_ref.at[slice_a], 13, 1)
    arrive(second_rx.at[1], 12)
    chosen_ref[slice_b, :] = total(first_sum[1, pl.ds(aligned(y * small, 16), small), :], second_rx.at[1])
    spread("y", chosen_ref.at[slice_b], lambda slot: chosen_ref.at[slice_b], 14, 1)
    send(features_ref, features_rx, 18, 2, partner)
    keep(chunks, 2 * chunks)
    arrive(chosen_ref.at[pl.ds(0, 3 * small)], 13)
    piece_a = pl.ds(aligned(base_a, 16), piece)
    spread("y", chosen_ref.at[piece_a], lambda slot: chosen_ref.at[piece_a], 15, 1)
    arrive(chosen_ref.at[pl.ds(0, 3 * small)], 14)
    piece_b = pl.ds(aligned(base_b, 16), piece)
    spread("z", chosen_ref.at[piece_b], lambda slot: chosen_ref.at[piece_b], 16, 1)
    arrive(square_ref.at[pl.ds(0, 7 * quarter)], 8)
    own_share = pl.ds(aligned(core * share, 16), share)

    def between(t):
        @pl.when(t == 1)
        def _():
            arrive(chosen_ref.at[pl.ds(0, 3 * piece)], 15)
            arrive(chosen_ref.at[pl.ds(0, 3 * piece)], 16)
            send(chosen_ref.at[own_share], chosen_ref.at[own_share], 17, 1, partner)

    state[...] = square_ref[...]
    invert(state, right, between)
    arrive(panel_ref.at[pl.ds(0, 3 * panel_piece)], 9)
    coeffs = jnp.dot(state[:, :count], panel_ref[...], precision=HIGHEST, preferred_element_type=f32)
    high[...] = coeffs.astype(bf16)
    low[...] = (coeffs - high[...].astype(f32)).astype(bf16)
    arrive(chosen_ref.at[pl.ds(0, share)], 17)

    def differ(index):
        spots = pl.ds(aligned(index * chunk, chunk), chunk)
        chosen = chosen_ref[spots, :][:, :count]
        change = jnp.dot(chosen, high[...], preferred_element_type=f32)
        change += jnp.dot(chosen, low[...], preferred_element_type=f32)
        wide = weight_ref[spots, :].astype(f32)
        masked = (wide - change) * kept[spots, :].astype(f32)
        pruned_ref[spots, :] = masked.astype(bf16)
        return (wide - masked).astype(bf16)

    def prepare_sent(k):
        spots = slice(k * chunk, (k + 1) * chunk)
        sent_diff[spots, :] = differ((1 - core) * chunks + k)
        send(sent_diff.at[spots], diff_rx.at[spots], 20 + k, 2, partner)

    def prepare_own(k):
        own_diff[k * chunk : (k + 1) * chunk, :] = differ(core * chunks + k)

    token_blocks = part.shape[1]

    def multiply(k):
        spots = slice(k * chunk, (k + 1) * chunk)
        tokens = features_ref.shape[0] // token_blocks

        @pl.loop(0, token_blocks)
        def _(t):
            words = pl.ds(aligned(t * tokens, tokens), tokens)
            product = lax.dot_general(
                features_ref[words, :], own_diff[spots, :], (((1,), (1,)), ((), ())), preferred_element_type=f32
            )
            product += lax.dot_general(
                features_rx[words, :], diff_rx[spots, :], (((1,), (1,)), ((), ())), preferred_element_type=f32
            )
            part[k, t] = product.astype(bf16).reshape(part.shape[2:])

    def ring(axis, parcel, value, extent, through_rx, through, rx, first):
        index, device = axes[axis]
        right_one, left_one, across = lax.rem(index + 1, 4), lax.rem(index + 3, 4), lax.rem(index + 2, 4)
        lo, hi = pl.ds(0, extent // 2), pl.ds(extent // 2, extent // 2)
        send(parcel(across).at[lo], through_rx.at[0], first, 3, device(right_one))
        send(parcel(across).at[hi], through_rx.at[1], first + 1, 3, device(left_one))
        send(parcel(right_one).at[hi], rx.at[0, hi], first + 2, 3, device(right_one))
        send(parcel(left_one).at[lo], rx.at[1, lo], first + 2, 3, device(left_one))

        def pass_on():
            arrive(through_rx.at[0], first)
            through[0] = (value(right_one, lo) + through_rx[0].astype(f32)).astype(bf16)
            send(through.at[0], rx.at[0, lo], first + 2, 3, device(right_one))
            arrive(through_rx.at[1], first + 1)
            through[1] = (value(left_one, hi) + through_rx[1].astype(f32)).astype(bf16)
            send(through.at[1], rx.at[1, hi], first + 2, 3, device(left_one))

        def finish():
            arrive(rx, first + 2)
            return value(index, pl.ds(0, extent)) + rx[0].astype(f32) + rx[1].astype(f32)

        return pass_on, finish

    order = [k for pair in zip(range(chunks // 2), range(chunks // 2, chunks)) for k in pair]
    rings = {}

    def reduce_first(k):
        if k == order[0]:
            arrive(features_rx, 18)
        arrive(diff_rx.at[k * chunk : (k + 1) * chunk], 20 + k)
        multiply(k)
        if k < chunks // 2:
            axis = "y"
            parcel = functools.partial(lambda k, j: part.at[k, j], k)
        else:
            axis = "z"
            parcel = functools.partial(lambda k, j: part.at[k, :, j], k)
        value = functools.partial(lambda parcel, j, which: parcel(j).at[which][...].astype(f32), parcel)
        rings[k] = ring(axis, parcel, value, 4, forward_rx.at[k], forward.at[k], ring_rx.at[k], 24 + 3 * k)

    for k in order:
        prepare_sent(k)
    prepare_own(order[0])
    prepare_own(order[1])
    for n, k in enumerate(order):
        reduce_first(k)
        if n + 2 < chunks:
            prepare_own(order[n + 2])
    for k in order:
        rings[k][0]()
    tokens = error_ref.shape[0]
    for k in order:
        value_sum = rings[k][1]()
        sums_wide[k] = value_sum
        sums[k] = value_sum.astype(bf16)
        index, device = axes["z" if k < chunks // 2 else "y"]
        for slot, peer, side in around(index):
            words = pl.ds(aligned(side * tokens, tokens), tokens)
            send(sums.at[k, peer, words], last_rx.at[k, slot], 24 + 3 * chunks + k, 3, device(peer, side))
    for k in order:
        index = axes["z" if k < chunks // 2 else "y"][0]
        arrive(last_rx.at[k], 24 + 3 * chunks + k)
        here_sum = sums_wide[k, index, pl.ds(aligned(core * tokens, tokens), tokens), :]
        there_sum = last_rx[k, 0].astype(f32)
        for step in (1, 2, 3):
            here_sum += last_rx[k, 2 * step - 1].astype(f32)
            there_sum += last_rx[k, 2 * step].astype(f32)
        error_ref[:, pl.ds(aligned(core * share + k * chunk, chunk), chunk)] = here_sum
        error_ref[:, pl.ds(aligned((1 - core) * share + k * chunk, chunk), chunk)] = there_sum
    unit_bytes = columns * jnp.dtype(weight_ref.dtype).itemsize
    for group, size in sent.items():
        view = weight_ref.at[pl.ds(0, size // unit_bytes)]
        remote(view, view, 0, group, partner).wait_send()


def prune(own_rows, line, limit, weight, mask, features, height):
    count, columns = own_rows.shape
    rows = weight.shape[0]
    tokens = features.shape[0]
    f32, bf16 = jnp.float32, jnp.bfloat16
    quarter = count // 8
    share, chunks = rows // 2, 4
    piece = share // 8
    small = piece // 4
    chunk = share // chunks
    vmem = pl.BlockSpec(memory_space=pltpu.VMEM)
    arrivals = 24 + 4 * chunks
    return pl.pallas_call(
        functools.partial(prune_kernel, height=height),
        out_shape=(
            jax.ShapeDtypeStruct((rows, columns), bf16),
            jax.ShapeDtypeStruct((tokens // 32, rows), f32),
        ),
        in_specs=[vmem] * 6,
        out_specs=(vmem, vmem),
        scratch_shapes=[
            pltpu.VMEM((rows, columns), bf16),
            pltpu.VMEM((16, rows), bf16),
            pltpu.VMEM((count, columns), f32),
            pltpu.VMEM((count, LANES), f32),
            pltpu.VMEM((7, quarter, LANES), f32),
            pltpu.VMEM((quarter, LANES), f32),
            pltpu.VMEM((3, quarter, LANES), f32),
            pltpu.VMEM((quarter, LANES), f32),
            pltpu.VMEM((3, quarter, LANES), f32),
            pltpu.VMEM((count, LANES), f32),
            pltpu.VMEM((count, LANES), f32),
            pltpu.VMEM((BLK, LANES), f32),
            pltpu.VMEM((3, count // 4, columns), f32),
            pltpu.VMEM((count, columns), f32),
            pltpu.VMEM((rows, LANES), bf16),
            pltpu.VMEM((share, LANES), bf16),
            pltpu.VMEM((share, LANES), bf16),
            pltpu.VMEM((2, 3, piece, LANES), bf16),
            pltpu.VMEM((2, piece, LANES), bf16),
            pltpu.VMEM((2, 3, small, LANES), bf16),
            pltpu.VMEM((rows, LANES), bf16),
            pltpu.VMEM((count, columns), bf16),
            pltpu.VMEM((count, columns), bf16),
            pltpu.VMEM(features.shape, bf16),
            pltpu.VMEM((share, columns), bf16),
            pltpu.VMEM((share, columns), bf16),
            pltpu.VMEM((share, columns), bf16),
            pltpu.VMEM((chunks, 4, 4, 64, chunk), bf16),
            pltpu.VMEM((chunks, 2, 2, 64, chunk), bf16),
            pltpu.VMEM((chunks, 2, 2, 64, chunk), bf16),
            pltpu.VMEM((chunks, 2, 4, 64, chunk), bf16),
            pltpu.VMEM((chunks, 4, 64, chunk), bf16),
            pltpu.VMEM((chunks, 4, 64, chunk), f32),
            pltpu.VMEM((chunks, 7, tokens // 32, chunk), bf16),
            pltpu.SemaphoreType.DMA((4,)),
            pltpu.SemaphoreType.DMA((arrivals,)),
        ],
        compiler_params=pltpu.CompilerParams(
            collective_id=0, has_side_effects=True, vmem_limit_bytes=32 << 20
        ),
        name="prune",
    )(own_rows, line, limit, weight, mask, features)


def local(weight, hess_inv, selected, block_mask, row_limits, calibration):
    rows_local = hess_inv.shape[0]
    row_offset = (lax.axis_index("rows") * rows_local).astype(jnp.int32).reshape(1)
    own_rows, line = gather(row_offset, selected, hess_inv)
    pruned, error = prune(
        own_rows, line, row_limits.reshape(1, -1), weight, block_mask, calibration, rows_local
    )
    return (pruned, error.T)


def solution(mesh):
    placed = (
        P("rows", "cols"),
        P("rows", "cols"),
        P(),
        P("rows", None),
        P("rows"),
        P(None, "cols"),
    )
    return jax.shard_map(
        local,
        mesh=mesh,
        in_specs=placed,
        out_specs=(P("rows", "cols"), P("rows", "cols")),
        check_vma=False,
    )
```
